32 devices in a mesh: grp: 2 (over x), seq: 8 (over z, y), ch: 2 (over core).
Axes of the slice: x: 2, y: 2, z: 4, core: 2. Of those that a mesh axis runs over, the one named last changes fastest.
Arguments:
- tokens: bfloat16 [16, 1024, 2048], P(('grp', 'seq'), None, 'ch'), parts along dimension 0, may hold values from -6 to 6
- short_weight: float32 [3, 2048], P(None, 'ch'), may hold values from -3 to 3
- inner_factor: bfloat16 [1024, 1024], P('seq'), may hold values from -0.1875 to 0.1875
- outer_factor: float32 [8, 8], replicated, may hold values from -2 to 2
- twiddle: float32 [8, 1024], P(None, 'seq'), may hold values from 0.5 to 1.5
- kernel: bfloat16 [8, 1024, 2048], P(None, 'seq', 'ch'), may hold values from -6 to 6
- cotangent: bfloat16 [16, 1024, 2048], P(('grp', 'seq'), None, 'ch'), parts along dimension 0, may hold values from -6 to 6
Outputs:
- mixer_out: bfloat16 [16, 1024, 2048], P(('grp', 'seq'), None, 'ch'), parts along dimension 0
- token_grad: bfloat16 [16, 1024, 2048], P(('grp', 'seq'), None, 'ch'), parts along dimension 0
- kernel_grad: bfloat16 [16, 1024, 2048], P('grp', 'seq', 'ch'), parts along dimension 0
The draws below stay inside these ranges and needn't reach their ends.
There are 2 independent parts, one for each index of `grp`. The reference program is written for one: setup_inputs(seed, part) draws one part's arguments, and reference() takes and returns one part's arrays. A program takes and returns all parts, laid end to end along the dimension named above; an argument that names none is the same for every part. Nothing has to cross between parts.
All inputs are finite; a program needn't handle non-finite values.
Results may differ from the reference program's by a relative error of at most 0.0064.
Values may be sent and summed in bfloat16 or wider, within the bound.
No kernel may reach another device: no remote copies, remote signals or barrier semaphores. Data moves between devices by JAX's collectives and lax.ppermute only.
A program may use at most 128 MiB of HBM per device.

```python
import jax
import jax.numpy as jnp
from jax import lax

D = 2048
BLOCK = 1024
BLOCKS = 8


def levels(stream_key, shape, split, least, largest):
    level, own = 1.0, jax.random.fold_in(stream_key, 6)
    for position, shards_of in split:
        draws = jnp.exp(jax.random.uniform(jax.random.fold_in(own, position), (shards_of,), jnp.float32, least / len(split), largest / len(split)))
        level = level * jnp.repeat(draws, shape[position] // shards_of).reshape([-1 if axis == position else 1 for axis in range(len(shape))])
    return level


def bell_draw(own_key, shape, scale, bound, shards=(), kind=jnp.bfloat16):
    values = jax.random.normal(own_key, shape, jnp.float32) * scale
    if len(shards) > 0:
        values = levels(own_key, shape, shards, -0.22, 0.18) * values
    return jnp.clip(values, min=-bound, max=bound).astype(kind)


def setup_inputs(seed: int = 0, part: int = 0) -> dict:
    key_list = jax.random.split(jax.random.key(seed), 8)
    part_splits = jax.random.split(jax.random.fold_in(key_list[7], part), 8)
    tokens = bell_draw(part_splits[0], (BLOCKS, BLOCK, D), 1.0, 6.0, ((0, 8), (2, 2)))
    short_weight = bell_draw(key_list[1], (3, D), 0.6, 3.0, ((1, 2),), jnp.float32)
    inner_factor = bell_draw(key_list[2], (BLOCK, BLOCK), BLOCK ** -0.5, 0.1875, ((0, 8),))
    outer_factor = bell_draw(key_list[3], (BLOCKS, BLOCKS), BLOCKS ** -0.5, 2.0, (), jnp.float32)
    twiddle = jnp.clip(0.5 + 1.0 * jax.random.uniform(key_list[4], (BLOCKS, BLOCK), jnp.float32) ** levels(key_list[4], (BLOCKS, BLOCK), ((1, 8),), -0.2, 0.2), 0.5, 1.5)
    kernel = bell_draw(key_list[5], (BLOCKS, BLOCK, D), 1.0, 6.0, ((1, 8), (2, 2)))
    cotangent = bell_draw(part_splits[6], (BLOCKS, BLOCK, D), 1.0, 6.0, ((0, 8), (2, 2)))
    return dict(tokens=tokens, short_weight=short_weight, inner_factor=inner_factor, outer_factor=outer_factor, twiddle=twiddle, kernel=kernel, cotangent=cotangent)


def block_terms(tokens, short_weight, inner_factor, outer_factor, twiddle, kernel, cotangent):
    blocks_all, block_size, channels = tokens.shape
    flat_tokens = tokens.astype(jnp.float32).reshape(blocks_all * block_size, channels)
    zero_rows = jnp.zeros((2, channels), jnp.float32)
    padded = jnp.concatenate([zero_rows, flat_tokens], axis=0)
    short_conv = short_weight[0] * padded[2:] + short_weight[1] * padded[1:-1] + short_weight[2] * padded[:-2]
    sigmoid_value = jax.nn.sigmoid(short_conv)
    gate_value = (short_conv * sigmoid_value).reshape(blocks_all, block_size, channels)
    slope_value = (sigmoid_value * (1.0 + short_conv * (1.0 - sigmoid_value))).reshape(blocks_all, block_size, channels)
    inner_wide = inner_factor.astype(jnp.float32)
    twiddle_wide = twiddle[:, :, None]
    kernel_wide = kernel.astype(jnp.float32)
    cot_wide = cotangent.astype(jnp.float32)
    spread = jnp.einsum("jk,ikc->ijc", inner_wide, tokens.astype(jnp.float32)).astype(jnp.bfloat16)
    forward_mid = jnp.einsum("ik,kjc->ijc", outer_factor, twiddle_wide * spread.astype(jnp.float32), precision=lax.Precision.HIGHEST)
    out_fwd = (twiddle_wide * jnp.einsum("ki,kjc->ijc", outer_factor, kernel_wide * forward_mid, precision=lax.Precision.HIGHEST)).astype(jnp.bfloat16)
    conv_out = jnp.einsum("kj,ikc->ijc", inner_wide, out_fwd.astype(jnp.float32))
    mixer_out = (gate_value * conv_out).astype(jnp.bfloat16)
    gated_cot = (cot_wide * gate_value).astype(jnp.bfloat16)
    short_grad = (cot_wide * conv_out * slope_value).reshape(blocks_all * block_size, channels)
    spread_cot = jnp.einsum("jk,ikc->ijc", inner_wide, gated_cot.astype(jnp.float32)).astype(jnp.bfloat16)
    back_mid = jnp.einsum("ik,kjc->ijc", outer_factor, twiddle_wide * spread_cot.astype(jnp.float32), precision=lax.Precision.HIGHEST)
    kernel_grad = (back_mid * forward_mid).astype(jnp.bfloat16)
    out_bwd = (twiddle_wide * jnp.einsum("ki,kjc->ijc", outer_factor, kernel_wide * back_mid, precision=lax.Precision.HIGHEST)).astype(jnp.bfloat16)
    extended = jnp.concatenate([short_grad, zero_rows], axis=0)
    back_short = short_weight[0] * extended[:-2] + short_weight[1] * extended[1:-1] + short_weight[2] * extended[2:]
    conv_back = jnp.einsum("kj,ikc->ijc", inner_wide, out_bwd.astype(jnp.float32))
    token_grad = (conv_back + back_short.reshape(blocks_all, block_size, channels)).astype(jnp.bfloat16)
    return mixer_out, token_grad, kernel_grad


def reference(tokens, short_weight, inner_factor, outer_factor, twiddle, kernel, cotangent):
    blocks_all, block_size, channels = tokens.shape
    block_width = min(channels, 512)
    block_count = channels // block_width

    def one_block(index):
        start = (index * block_width).astype(jnp.int32)
        local_tokens = lax.dynamic_slice_in_dim(tokens, start, block_width, 2)
        local_taps = lax.dynamic_slice_in_dim(short_weight, start, block_width, 1)
        local_kernel = lax.dynamic_slice_in_dim(kernel, start, block_width, 2)
        local_cot = lax.dynamic_slice_in_dim(cotangent, start, block_width, 2)
        return block_terms(local_tokens, local_taps, inner_factor, outer_factor, twiddle, local_kernel, local_cot)

    stacked = lax.map(one_block, jnp.arange(block_count, dtype=jnp.int32))

    def unstack(pieces):
        return jnp.moveaxis(pieces, 0, 2).reshape(blocks_all, block_size, channels)

    return unstack(stacked[0]), unstack(stacked[1]), unstack(stacked[2])
```

```python
import functools

import jax
import jax.numpy as jnp
from jax import lax
from jax.experimental import pallas as pl
from jax.experimental.pallas import tpu as pltpu
from jax.sharding import PartitionSpec as P

BF16, F32 = jnp.bfloat16, jnp.float32
VMEM_LIMIT = 48 * 1024 * 1024


def hop(block, distance):
    peers = lax.axis_size("seq")
    return lax.ppermute(block, "seq", [(i, (i + distance) % peers) for i in range(peers)])


def shifted(block, distance):
    devices = range(lax.axis_size("seq"))
    return lax.ppermute(block, "seq", [(i - distance, i) for i in devices if i - distance in devices])


def swap_cores(block):
    return lax.ppermute(block, "ch", [(0, 1), (1, 0)])


def call(body, name, grid, in_specs, out_specs, out_shape, flops, moved, scalars=0, transcendentals=0):
    return pl.pallas_call(
        body,
        name=name,
        grid_spec=pltpu.PrefetchScalarGridSpec(
            num_scalar_prefetch=scalars, grid=grid, in_specs=in_specs, out_specs=out_specs
        ),
        out_shape=out_shape,
        compiler_params=pltpu.CompilerParams(vmem_limit_bytes=VMEM_LIMIT),
        cost_estimate=pl.CostEstimate(flops=flops, bytes_accessed=moved, transcendentals=transcendentals),
    )


def whole(shape):
    return pl.BlockSpec(shape, lambda c, *_: (0,) * len(shape))


def tile(rows, width):
    return pl.BlockSpec((rows, width), lambda c, *_: (0, c))


def struct(shape, dtype):
    return jax.ShapeDtypeStruct(shape, dtype)


def matmul(left, right):
    return jnp.dot(left, right, preferred_element_type=F32)


def gate_body(tokens, halo, weight, cot, gated, gate, scaled):
    x = tokens[...].astype(F32)
    row = lax.broadcasted_iota(jnp.int32, x.shape, 0)
    edge = halo[...].astype(F32)
    one_back = jnp.where(row == 0, edge[1:2], pltpu.roll(x, 1, 0))
    two_back = jnp.where(row == 0, edge[0:1], jnp.where(row == 1, edge[1:2], pltpu.roll(x, 2, 0)))
    taps = weight[...]
    conv = taps[0:1] * x + taps[1:2] * one_back + taps[2:3] * two_back
    sig = jax.nn.sigmoid(conv)
    value = conv * sig
    slope = sig * (1.0 + conv * (1.0 - sig))
    wide = cot[...].astype(F32)
    gated[...] = (wide * value).astype(BF16)
    gate[...] = value
    scaled[...] = wide * slope


def gate_call(tokens, halo, weight, cot):
    length, channels = tokens.shape
    width = min(channels, 128)
    return call(
        gate_body,
        "gate",
        (channels // width,),
        [tile(length, width), tile(2, width), tile(3, width), tile(length, width)],
        [tile(length, width)] * 3,
        [struct((length, channels), BF16), struct((length, channels), F32), struct((length, channels), F32)],
        20 * length * channels,
        14 * length * channels,
        transcendentals=2 * length * channels,
    )(tokens, halo, weight, cot)


def spread_first_body(peers, core, own, *refs):
    mine, other = refs[: peers - 1], refs[peers - 1 : 2 * peers - 2]
    values, joined, pieces = refs[2 * peers - 2], refs[2 * peers - 1], refs[2 * peers :]
    share = own.shape[0]
    half = share // 2

    @pl.when(pl.program_id(0) == 0)
    def _():
        joined[0:share] = own[...]

        @pl.when(core[0] == 0)
        def _():
            for k in range(1, peers):
                joined[k * share : k * share + half] = mine[k - 1][...]
                joined[k * share + half : (k + 1) * share] = other[k - 1][...]

        @pl.when(core[0] != 0)
        def _():
            for k in range(1, peers):
                joined[k * share : k * share + half] = other[k - 1][...]
                joined[k * share + half : (k + 1) * share] = mine[k - 1][...]

    spread_pieces(joined, values, pieces)


def spread_pieces(joined, values, pieces):
    share = pieces[0].shape[0]
    product = matmul(joined[...], values[...]).astype(BF16)
    for k, piece in enumerate(pieces):
        piece[...] = product[k * share : (k + 1) * share]


def spread_body(joined, values, *pieces):
    spread_pieces(joined, values, pieces)


def spread_first_call(core, own, mine, other, values):
    share, block = own.shape
    channels = values.shape[1]
    peers = len(mine) + 1
    width = min(channels, 256)
    halves = [whole((share // 2, block))] * (2 * peers - 2)
    out = call(
        functools.partial(spread_first_body, peers),
        "spread_first",
        (channels // width,),
        [whole((share, block))] + halves + [tile(block, width)],
        [whole((peers * share, block))] + [tile(share, width)] * peers,
        [struct((peers * share, block), BF16)] + [struct((share, channels), BF16)] * peers,
        2 * block * block * channels,
        4 * block * channels + 4 * block * block,
        scalars=1,
    )(core, own, *mine, *other, values)
    return out[0], list(out[1:])


def spread_call(joined, values, peers):
    block, channels = values.shape
    share = block // peers
    width = min(channels, 256)
    return list(
        call(
            spread_body,
            "spread",
            (channels // width,),
            [whole((block, block)), tile(block, width)],
            [tile(share, width)] * peers,
            [struct((share, channels), BF16)] * peers,
            2 * block * block * channels,
            4 * block * channels + 2 * block * block,
        )(joined, values)
    )


def turn_body(joined, turned):
    turned[...] = joined[...].T


def turn_call(joined):
    block = joined.shape[0]
    width = min(block, 256)
    return call(
        turn_body,
        "turn",
        (block // width,),
        [tile(block, width)],
        pl.BlockSpec((width, block), lambda c: (c, 0)),
        struct((block, block), BF16),
        block * block,
        4 * block * block,
    )(joined)


def two_part(values):
    high = values.astype(BF16)
    return high, (values - high.astype(F32)).astype(BF16)


def middle_body(peers, span, with_grad, place, high, low, high_t, low_t, kern, *refs):
    pieces, refs = refs[:peers], refs[peers:]
    if with_grad:
        first, refs = refs[:peers], refs[peers:]
        grad, refs = refs[0], refs[1:]
    outs = refs[:peers]
    columns = pieces[0].shape[0]
    rows = [lax.rem(place[0] + r, peers) for r in range(peers)]
    for g in range(columns // span):
        part = slice(g * span, (g + 1) * span)
        stacked = jnp.concatenate([piece[part] for piece in pieces], axis=0)
        mid = matmul(high[g], stacked) + matmul(low[g], stacked)
        if with_grad:
            stacked = jnp.concatenate([piece[part] for piece in first], axis=0)
            product = ((matmul(high[g], stacked) + matmul(low[g], stacked)) * mid).astype(BF16)
            for r in range(peers):
                grad[rows[r], part] = product[r * span : (r + 1) * span]
        filters = jnp.concatenate([kern[rows[r], part] for r in range(peers)], axis=0)
        upper, lower = two_part(filters.astype(F32) * mid)
        result = matmul(high_t[g], upper) + matmul(low_t[g], upper) + matmul(high_t[g], lower)
        result = result.astype(BF16)
        for r in range(peers):
            outs[r][part] = result[r * span : (r + 1) * span]


def middle_call(place, factors, kern, pieces, first=None):
    peers, columns, channels = kern.shape
    groups, side, _ = factors[0].shape
    width = min(channels, 256)
    cube = pl.BlockSpec((peers, columns, width), lambda c, *_: (0, 0, c))
    with_grad = first is not None
    n_in = peers * (2 if with_grad else 1)
    out = call(
        functools.partial(middle_body, peers, side // peers, with_grad),
        "middle_grad" if with_grad else "middle",
        (channels // width,),
        [whole((groups, side, side))] * 4 + [cube] + [tile(columns, width)] * n_in,
        ([cube] if with_grad else []) + [tile(columns, width)] * peers,
        ([struct(kern.shape, BF16)] if with_grad else []) + [struct((columns, channels), BF16)] * peers,
        (14 if with_grad else 10) * groups * side * side * channels,
        (10 if with_grad else 6) * peers * columns * channels + 8 * groups * side * side,
        scalars=1,
    )(place, *factors, kern, *pieces, *(first or []))
    return (out[0], list(out[1:])) if with_grad else list(out)


def middle_factors(outer, twiddle, place):
    peers, columns = twiddle.shape
    span = min(columns, max(16, 256 // peers))
    groups, side = columns // span, peers * span
    outer_here = lax.dynamic_slice(jnp.tile(outer, (2, 2)), (place, place), (peers, peers))
    twiddle_here = lax.dynamic_slice(jnp.tile(twiddle, (2, 1)), (place, 0), (peers, columns))
    wide = jnp.repeat(jnp.repeat(outer_here, span, axis=0), span, axis=1)
    spot = jnp.arange(side) % span
    wide = jnp.where(spot[:, None] == spot[None, :], wide, 0.0)
    scale = twiddle_here.reshape(peers, groups, span).transpose(1, 0, 2).reshape(groups, 1, side)
    factor = wide[None] * scale
    high = lax.reduce_precision(factor, 8, 7)
    low = factor - high
    high, low = high.astype(BF16), low.astype(BF16)
    return high, low, high.transpose(0, 2, 1), low.transpose(0, 2, 1)


def join_rows(pieces):
    return jnp.concatenate([piece[...] for piece in pieces], axis=0)


def forward_body(peers, turned, weight, gate, scaled, *refs):
    pieces, (mixed, back, head) = refs[:peers], refs[peers:]
    conv = matmul(turned[...], join_rows(pieces))
    mixed[...] = (gate[...] * conv).astype(BF16)
    grad = scaled[...] * conv
    head[...] = grad[0:2]
    length = grad.shape[0]
    row = lax.broadcasted_iota(jnp.int32, grad.shape, 0)
    taps = weight[...]
    one_on = jnp.where(row < length - 1, pltpu.roll(grad, length - 1, 0), 0.0)
    two_on = jnp.where(row < length - 2, pltpu.roll(grad, length - 2, 0), 0.0)
    back[...] = taps[0:1] * grad + taps[1:2] * one_on + taps[2:3] * two_on


def forward_call(turned, weight, gate, scaled, pieces):
    length, channels = gate.shape
    peers, share = len(pieces), pieces[0].shape[0]
    width = min(channels, 256)
    return call(
        functools.partial(forward_body, peers),
        "forward_rows",
        (channels // width,),
        [whole(turned.shape), tile(3, width), tile(length, width), tile(length, width)]
        + [tile(share, width)] * peers,
        [tile(length, width), tile(length, width), tile(2, width)],
        [struct((length, channels), BF16), struct((length, channels), F32), struct((2, channels), F32)],
        2 * length * length * channels,
        16 * length * channels + 2 * length * length,
    )(turned, weight, gate, scaled, *pieces)


def backward_body(peers, turned, weight, back, tail, *refs):
    pieces, grad = refs[:peers], refs[peers]
    total = matmul(turned[...], join_rows(pieces)) + back[...]
    taps, edge = weight[...], tail[...]
    length = total.shape[0]
    grad[...] = total.astype(BF16)
    last = total[length - 16 :]
    row = lax.broadcasted_iota(jnp.int32, last.shape, 0)
    extra = jnp.where(row == 15, taps[1:2] * edge[0:1] + taps[2:3] * edge[1:2], 0.0)
    extra = jnp.where(row == 14, taps[2:3] * edge[0:1], extra)
    grad[length - 16 :] = (last + extra).astype(BF16)


def backward_call(turned, weight, back, tail, pieces):
    length, channels = back.shape
    peers, share = len(pieces), pieces[0].shape[0]
    width = min(channels, 256)
    return call(
        functools.partial(backward_body, peers),
        "backward_rows",
        (channels // width,),
        [whole(turned.shape), tile(3, width), tile(length, width), tile(2, width)]
        + [tile(share, width)] * peers,
        tile(length, width),
        struct((length, channels), BF16),
        2 * length * length * channels,
        8 * length * channels + 2 * length * length,
    )(turned, weight, back, tail, *pieces)


def to_middle(pieces):
    return [piece if r == 0 else hop(piece, -r) for r, piece in enumerate(pieces)]


def to_rows(pieces):
    return [piece if r == 0 else hop(piece, r) for r, piece in enumerate(pieces)]


def on_device(tokens, short_weight, inner_factor, outer_factor, twiddle, kernel, cotangent):
    peers = lax.axis_size("seq")
    place, core = lax.axis_index("seq"), lax.axis_index("ch")
    row_count, block, channels = tokens.shape
    assert row_count == 1 and lax.axis_size("ch") == 2
    flat, cot = tokens.reshape(block, channels), cotangent.reshape(block, channels)
    share = inner_factor.shape[0]
    place_ref, core_ref = place.reshape(1).astype(jnp.int32), core.reshape(1).astype(jnp.int32)

    half = lax.dynamic_slice(inner_factor, (core * (share // 2), 0), (share // 2, block))
    mine = [hop(half, k) for k in range(1, peers)]
    other = [swap_cores(piece) for piece in mine]

    preceding = shifted(flat[-2:], 1)
    gated, gate, scaled = gate_call(flat, preceding, short_weight, cot)
    factors = middle_factors(outer_factor, twiddle, place)

    joined, spread = spread_first_call(core_ref, inner_factor, mine, other, flat)
    spread = to_middle(spread)
    spread_cot = to_middle(spread_call(joined, gated, peers))
    turned = turn_call(joined)

    rows_fwd = to_rows(middle_call(place_ref, factors, kernel, spread))
    kernel_grad, rows_bwd = middle_call(place_ref, factors, kernel, spread_cot, spread)
    rows_bwd = to_rows(rows_bwd)

    mixer_out, back, head = forward_call(turned, short_weight, gate, scaled, rows_fwd)
    following = shifted(head, -1)
    token_grad = backward_call(turned, short_weight, back, following, rows_bwd)
    return mixer_out.reshape(tokens.shape), token_grad.reshape(tokens.shape), kernel_grad


def solution(mesh):
    in_specs = (
        P(("grp", "seq"), None, "ch"),
        P(None, "ch"),
        P("seq", None),
        P(),
        P(None, "seq"),
        P(None, "seq", "ch"),
        P(("grp", "seq"), None, "ch"),
    )
    out_specs = (
        P(("grp", "seq"), None, "ch"),
        P(("grp", "seq"), None, "ch"),
        P("grp", "seq", "ch"),
    )
    return jax.shard_map(
        on_device, mesh=mesh, in_specs=in_specs, out_specs=out_specs, check_vma=False
    )
```

```python
import functools

import jax
import jax.numpy as jnp
from jax import lax
from jax.experimental import pallas as pl
from jax.experimental.pallas import tpu as pltpu
from jax.sharding import PartitionSpec as P

BF16, F32 = jnp.bfloat16, jnp.float32
VMEM_LIMIT = 48 * 1024 * 1024


def exchange(block, mask):
    return lax.ppermute(block, "seq", [(i, i ^ mask) for i in range(lax.axis_size("seq"))])


def shifted(block, distance):
    devices = range(lax.axis_size("seq"))
    return lax.ppermute(block, "seq", [(i - distance, i) for i in devices if i - distance in devices])


def swap_cores(block):
    return lax.ppermute(block, "ch", [(0, 1), (1, 0)])


def call(body, name, grid, in_specs, out_specs, out_shape, flops, moved, scalars=0, transcendentals=0):
    return pl.pallas_call(
        body,
        name=name,
        grid_spec=pltpu.PrefetchScalarGridSpec(
            num_scalar_prefetch=scalars, grid=grid, in_specs=in_specs, out_specs=out_specs
        ),
        out_shape=out_shape,
        compiler_params=pltpu.CompilerParams(vmem_limit_bytes=VMEM_LIMIT),
        cost_estimate=pl.CostEstimate(flops=flops, bytes_accessed=moved, transcendentals=transcendentals),
    )


def whole(shape):
    return pl.BlockSpec(shape, lambda c, *_: (0,) * len(shape))


def tile(rows, width):
    return pl.BlockSpec((rows, width), lambda c, *_: (0, c))


def struct(shape, dtype):
    return jax.ShapeDtypeStruct(shape, dtype)


def matmul(left, right):
    return jnp.dot(left, right, preferred_element_type=F32)


def gate_values(tokens, halo, weight):
    x = tokens[...].astype(F32)
    row = lax.broadcasted_iota(jnp.int32, x.shape, 0)
    edge, taps = halo[...].astype(F32), weight[...]
    one_back = jnp.where(row == 0, edge[1:2], pltpu.roll(x, 1, 0))
    two_back = jnp.where(row == 0, edge[0:1], jnp.where(row == 1, edge[1:2], pltpu.roll(x, 2, 0)))
    conv = taps[0:1] * x + taps[1:2] * one_back + taps[2:3] * two_back
    return conv, jax.nn.sigmoid(conv)


def spread_peer_body(core, mine, other, values, piece, rows):
    half = mine.shape[0]
    ours, theirs = matmul(mine[...], values[...]).astype(BF16), matmul(other[...], values[...]).astype(BF16)

    @pl.when(core[0] == 0)
    def _():
        piece[0:half], piece[half:] = ours, theirs
        rows[0:half], rows[half:] = mine[...], other[...]

    @pl.when(core[0] != 0)
    def _():
        piece[0:half], piece[half:] = theirs, ours
        rows[0:half], rows[half:] = other[...], mine[...]


def spread_peer_call(core, mine, other, values):
    half, block = mine.shape
    channels = values.shape[1]
    width = min(channels, 512)
    return call(
        spread_peer_body,
        "spread_peer",
        (channels // width,),
        [whole((half, block))] * 2 + [tile(block, width)],
        [tile(2 * half, width), whole((2 * half, block))],
        [struct((2 * half, channels), BF16), struct((2 * half, block), BF16)],
        4 * half * block * channels,
        2 * block * channels + 8 * half * block,
        scalars=1,
    )(core, mine, other, values)


def spread_own_body(row, values, piece):
    piece[...] = matmul(row[...], values[...]).astype(BF16)


def spread_own_call(row, values):
    share, block = row.shape
    channels = values.shape[1]
    width = min(channels, 512)
    return call(
        spread_own_body,
        "spread_own",
        (channels // width,),
        [whole((share, block)), tile(block, width)],
        tile(share, width),
        struct((share, channels), BF16),
        2 * share * block * channels,
        2 * block * channels + 2 * share * (block + channels),
    )(row, values)


def spread_gated_body(peers, tokens, halo, weight, cot, *refs):
    rows, pieces = refs[:peers], refs[peers:]
    conv, sig = gate_values(tokens, halo, weight)
    gated = (cot[...].astype(F32) * (conv * sig)).astype(BF16)
    for row, piece in zip(rows, pieces):
        piece[...] = matmul(row[...], gated).astype(BF16)


def spread_gated_call(tokens, halo, weight, cot, rows):
    block, channels = tokens.shape
    peers, share = len(rows), rows[0].shape[0]
    width = min(channels, 128)
    out = call(
        functools.partial(spread_gated_body, peers),
        "spread_gated",
        (channels // width,),
        [tile(block, width), tile(2, width), tile(3, width), tile(block, width)]
        + [whole((share, block))] * peers,
        [tile(share, width)] * peers,
        [struct((share, channels), BF16)] * peers,
        2 * peers * share * block * channels,
        4 * block * channels + 2 * peers * share * (block + channels),
        transcendentals=2 * block * channels,
    )(tokens, halo, weight, cot, *rows)
    return list(out)


def turn_body(peers, *refs):
    refs[peers][...] = join_rows(refs[:peers]).T


def turn_call(rows):
    share, block = rows[0].shape
    width = min(block, 256)
    return call(
        functools.partial(turn_body, len(rows)),
        "turn",
        (block // width,),
        [tile(share, width)] * len(rows),
        pl.BlockSpec((width, block), lambda c: (c, 0)),
        struct((block, block), BF16),
        block * block,
        4 * block * block,
    )(*rows)


def two_part(values):
    high = values.astype(BF16)
    return high, (values - high.astype(F32)).astype(BF16)


def middle_body(peers, span, with_grad, place, high, low, high_t, low_t, kern, *refs):
    pieces, refs = refs[:peers], refs[peers:]
    if with_grad:
        first, refs = refs[:peers], refs[peers:]
        grad, refs = refs[0], refs[1:]
    outs = refs[:peers]
    columns = pieces[0].shape[0]
    rows = [lax.bitwise_xor(place[0], r) for r in range(peers)]
    for g in range(columns // span):
        part = slice(g * span, (g + 1) * span)
        stacked = jnp.concatenate([piece[part] for piece in pieces], axis=0)
        mid = matmul(high[g], stacked) + matmul(low[g], stacked)
        if with_grad:
            stacked = jnp.concatenate([piece[part] for piece in first], axis=0)
            product = ((matmul(high[g], stacked) + matmul(low[g], stacked)) * mid).astype(BF16)
            for r in range(peers):
                grad[rows[r], part] = product[r * span : (r + 1) * span]
        filters = jnp.concatenate([kern[rows[r], part] for r in range(peers)], axis=0)
        upper, lower = two_part(filters.astype(F32) * mid)
        result = matmul(high_t[g], upper) + matmul(low_t[g], upper) + matmul(high_t[g], lower)
        result = result.astype(BF16)
        for r in range(peers):
            outs[r][part] = result[r * span : (r + 1) * span]


def middle_call(place, factors, kern, pieces, first=None):
    peers, columns, channels = kern.shape
    groups, side, _ = factors[0].shape
    width = min(channels, 256)
    cube = pl.BlockSpec((peers, columns, width), lambda c, *_: (0, 0, c))
    with_grad = first is not None
    n_in = peers * (2 if with_grad else 1)
    out = call(
        functools.partial(middle_body, peers, side // peers, with_grad),
        "middle_grad" if with_grad else "middle",
        (channels // width,),
        [whole((groups, side, side))] * 4 + [cube] + [tile(columns, width)] * n_in,
        ([cube] if with_grad else []) + [tile(columns, width)] * peers,
        ([struct(kern.shape, BF16)] if with_grad else []) + [struct((columns, channels), BF16)] * peers,
        (14 if with_grad else 10) * groups * side * side * channels,
        (10 if with_grad else 6) * peers * columns * channels + 8 * groups * side * side,
        scalars=1,
    )(place, *factors, kern, *pieces, *(first or []))
    return (out[0], list(out[1:])) if with_grad else list(out)


def middle_factors(outer, twiddle, place):
    peers, columns = twiddle.shape
    span = min(columns, max(16, 256 // peers))
    groups, side = columns // span, peers * span
    order = lax.bitwise_xor(jnp.arange(peers), place)
    pick = (order[:, None] == jnp.arange(peers)[None, :]).astype(F32)
    exact = functools.partial(jnp.dot, precision=lax.Precision.HIGHEST, preferred_element_type=F32)
    outer_here, twiddle_here = exact(exact(pick, outer), pick.T), exact(pick, twiddle)
    wide = jnp.repeat(jnp.repeat(outer_here, span, axis=0), span, axis=1)
    spot = jnp.arange(side) % span
    wide = jnp.where(spot[:, None] == spot[None, :], wide, 0.0)
    scale = twiddle_here.reshape(peers, groups, span).transpose(1, 0, 2).reshape(groups, 1, side)
    factor = wide[None] * scale
    high = lax.reduce_precision(factor, 8, 7)
    low = factor - high
    high, low = high.astype(BF16), low.astype(BF16)
    return high, low, high.transpose(0, 2, 1), low.transpose(0, 2, 1)


def join_rows(pieces):
    return jnp.concatenate([piece[...] for piece in pieces], axis=0)


def forward_body(peers, turned, weight, tokens, halo, cot, *refs):
    pieces, (mixed, back, head) = refs[:peers], refs[peers:]
    conv_out = matmul(turned[...], join_rows(pieces))
    conv, sig = gate_values(tokens, halo, weight)
    mixed[...] = (conv * sig * conv_out).astype(BF16)
    slope = sig * (1.0 + conv * (1.0 - sig))
    grad = cot[...].astype(F32) * conv_out * slope
    head[...] = grad[0:2]
    length = grad.shape[0]
    row = lax.broadcasted_iota(jnp.int32, grad.shape, 0)
    taps = weight[...]
    one_on = jnp.where(row < length - 1, pltpu.roll(grad, length - 1, 0), 0.0)
    two_on = jnp.where(row < length - 2, pltpu.roll(grad, length - 2, 0), 0.0)
    back[...] = taps[0:1] * grad + taps[1:2] * one_on + taps[2:3] * two_on


def forward_call(turned, weight, tokens, halo, cot, pieces):
    length, channels = tokens.shape
    peers, share = len(pieces), pieces[0].shape[0]
    width = min(channels, 128)
    return call(
        functools.partial(forward_body, peers),
        "forward_rows",
        (channels // width,),
        [whole(turned.shape), tile(3, width), tile(length, width), tile(2, width), tile(length, width)]
        + [tile(share, width)] * peers,
        [tile(length, width), tile(length, width), tile(2, width)],
        [struct((length, channels), BF16), struct((length, channels), F32), struct((2, channels), F32)],
        2 * length * length * channels,
        12 * length * channels + 2 * length * length,
        transcendentals=2 * length * channels,
    )(turned, weight, tokens, halo, cot, *pieces)


def partial_body(peers, turned, back, *refs):
    pieces, total = refs[:peers], refs[peers]
    total[...] = matmul(turned[...], join_rows(pieces)) + back[...]


def partial_call(turned, back, pieces):
    length, channels = back.shape
    peers, share = len(pieces), pieces[0].shape[0]
    width = min(channels, 256)
    depth = peers * share
    return call(
        functools.partial(partial_body, peers),
        "backward_part",
        (channels // width,),
        [pl.BlockSpec((length, depth), lambda c: (0, 0)), tile(length, width)]
        + [tile(share, width)] * peers,
        tile(length, width),
        struct((length, channels), F32),
        2 * length * depth * channels,
        8 * length * channels + 2 * length * depth + 2 * depth * channels,
    )(turned, back, *pieces)


def backward_body(peers, turned, weight, back, tail, *refs):
    pieces, grad = refs[:peers], refs[peers]
    total = matmul(turned[...], join_rows(pieces)) + back[...]
    taps, edge = weight[...], tail[...]
    length = total.shape[0]
    grad[...] = total.astype(BF16)
    last = total[length - 16 :]
    row = lax.broadcasted_iota(jnp.int32, last.shape, 0)
    extra = jnp.where(row == 15, taps[1:2] * edge[0:1] + taps[2:3] * edge[1:2], 0.0)
    extra = jnp.where(row == 14, taps[2:3] * edge[0:1], extra)
    grad[length - 16 :] = (last + extra).astype(BF16)


def backward_call(turned, weight, back, tail, pieces):
    length, channels = back.shape
    peers, share = len(pieces), pieces[0].shape[0]
    width = min(channels, 256)
    depth = peers * share
    last = turned.shape[1] // depth - 1
    return call(
        functools.partial(backward_body, peers),
        "backward_rows",
        (channels // width,),
        [pl.BlockSpec((length, depth), lambda c: (0, last)), tile(3, width), tile(length, width), tile(2, width)]
        + [tile(share, width)] * peers,
        tile(length, width),
        struct((length, channels), BF16),
        2 * length * depth * channels,
        6 * length * channels + 2 * length * depth + 2 * depth * channels,
    )(turned, weight, back, tail, *pieces)


def after(value, *others):
    return lax.optimization_barrier((value, *others))[0]


class Wire:
    DEPTH = 5

    def __init__(self):
        self.ended = []

    def exchange(self, block, mask):
        if len(self.ended) >= self.DEPTH:
            block = after(block, self.ended[-self.DEPTH])
        self.ended.append(exchange(block, mask))
        return self.ended[-1]


def on_device(tokens, short_weight, inner_factor, outer_factor, twiddle, kernel, cotangent):
    peers = lax.axis_size("seq")
    place, core = lax.axis_index("seq"), lax.axis_index("ch")
    row_count, block, channels = tokens.shape
    assert row_count == 1 and lax.axis_size("ch") == 2
    flat, cot = tokens.reshape(block, channels), cotangent.reshape(block, channels)
    share = inner_factor.shape[0]
    place_ref, core_ref = place.reshape(1).astype(jnp.int32), core.reshape(1).astype(jnp.int32)
    assert peers & (peers - 1) == 0
    far = peers // 2
    others = [far] + [m for pair in zip(range(1, far), range(far + 1, peers)) for m in pair]
    arrival = [0] + others
    wire = Wire()

    half = lax.dynamic_slice(inner_factor, (core * (share // 2), 0), (share // 2, block))
    mine = {far: wire.exchange(half, far)}
    for m in range(1, far):
        mine[m] = wire.exchange(half, m)
    preceding = shifted(flat[-2:], 1)
    for m in range(1, far):
        mine[far + m] = wire.exchange(mine[far], m)

    rows, spread, pieces = {0: inner_factor}, {}, []
    for m in others:
        piece, rows[m] = spread_peer_call(core_ref, mine[m], swap_cores(mine[m]), flat)
        pieces.append(piece)
        spread[m] = wire.exchange(piece, m)
    held = after(flat, pieces[-1])
    spread[0] = spread_own_call(inner_factor, held)

    factors = middle_factors(outer_factor, twiddle, place)
    in_order = [rows[m] for m in range(peers)]
    spread_cot = spread_gated_call(held, preceding, short_weight, cot, in_order)
    spread_cot = {m: wire.exchange(spread_cot[m], m) for m in others} | {0: spread_cot[0]}
    turned = turn_call([rows[m] for m in arrival])

    spread = [spread[m] for m in range(peers)]
    mid = middle_call(place_ref, factors, kernel, spread)
    rows_fwd = {m: wire.exchange(mid[m], m) for m in others} | {0: mid[0]}
    spread_cot[0] = after(spread_cot[0], mid[0])
    kernel_grad, mid = middle_call(place_ref, factors, kernel, [spread_cot[m] for m in range(peers)], spread)
    rows_bwd = {m: wire.exchange(mid[m], m) for m in others} | {0: mid[0]}

    mixer_out, back, head = forward_call(
        turned, short_weight, flat, preceding, cot, [rows_fwd[m] for m in arrival]
    )
    following = shifted(head, -1)
    late = max(1, peers // 4)
    back = partial_call(turned, back, [rows_bwd[m] for m in arrival[:-late]])
    token_grad = backward_call(turned, short_weight, back, following, [rows_bwd[m] for m in arrival[-late:]])
    return mixer_out.reshape(tokens.shape), token_grad.reshape(tokens.shape), kernel_grad


def solution(mesh):
    in_specs = (
        P(("grp", "seq"), None, "ch"),
        P(None, "ch"),
        P("seq", None),
        P(),
        P(None, "seq"),
        P(None, "seq", "ch"),
        P(("grp", "seq"), None, "ch"),
    )
    out_specs = (
        P(("grp", "seq"), None, "ch"),
        P(("grp", "seq"), None, "ch"),
        P("grp", "seq", "ch"),
    )
    return jax.shard_map(
        on_device, mesh=mesh, in_specs=in_specs, out_specs=out_specs, check_vma=False
    )
```

```python
import functools

import jax
import jax.numpy as jnp
from jax import lax
from jax.experimental import pallas as pl
from jax.experimental.pallas import tpu as pltpu
from jax.sharding import PartitionSpec as P

BF16, F32 = jnp.bfloat16, jnp.float32
MIB = 1024 * 1024
VMEM_LIMIT = 48 * MIB


def exchange(block, mask):
    return lax.ppermute(block, "seq", [(i, i ^ mask) for i in range(lax.axis_size("seq"))])


def shifted(block, distance):
    devices = range(lax.axis_size("seq"))
    return lax.ppermute(block, "seq", [(i - distance, i) for i in devices if i - distance in devices])


def swap_cores(block):
    return lax.ppermute(block, "ch", [(0, 1), (1, 0)])


def call(body, name, grid, in_specs, out_specs, out_shape, flops, moved, scalars=0, transcendentals=0):
    return pl.pallas_call(
        body,
        name=name,
        grid_spec=pltpu.PrefetchScalarGridSpec(
            num_scalar_prefetch=scalars, grid=grid, in_specs=in_specs, out_specs=out_specs
        ),
        out_shape=out_shape,
        compiler_params=pltpu.CompilerParams(vmem_limit_bytes=VMEM_LIMIT),
        cost_estimate=pl.CostEstimate(flops=flops, bytes_accessed=moved, transcendentals=transcendentals),
    )


def whole(shape):
    return pl.BlockSpec(shape, lambda c, *_: (0,) * len(shape))


def tile(rows, width):
    return pl.BlockSpec((rows, width), lambda c, *_: (0, c))


def struct(shape, dtype):
    return jax.ShapeDtypeStruct(shape, dtype)


def matmul(left, right):
    return jnp.dot(left, right, preferred_element_type=F32)


def gate_values(tokens, halo, weight):
    x = tokens[...].astype(F32)
    row = lax.broadcasted_iota(jnp.int32, x.shape, 0)
    edge, taps = halo[...].astype(F32), weight[...]
    one_back = jnp.where(row == 0, edge[1:2], pltpu.roll(x, 1, 0))
    two_back = jnp.where(row == 0, edge[0:1], jnp.where(row == 1, edge[1:2], pltpu.roll(x, 2, 0)))
    conv = taps[0:1] * x + taps[1:2] * one_back + taps[2:3] * two_back
    return conv, jax.nn.sigmoid(conv)


def spread_peer_body(core, mine, other, values, piece, rows):
    half = mine.shape[0]
    ours, theirs = matmul(mine[...], values[...]).astype(BF16), matmul(other[...], values[...]).astype(BF16)

    @pl.when(core[0] == 0)
    def _():
        piece[0:half], piece[half:] = ours, theirs
        rows[0:half], rows[half:] = mine[...], other[...]

    @pl.when(core[0] != 0)
    def _():
        piece[0:half], piece[half:] = theirs, ours
        rows[0:half], rows[half:] = other[...], mine[...]


def spread_peer_call(core, mine, other, values):
    half, block = mine.shape
    channels = values.shape[1]
    width = min(channels, 512)
    return call(
        spread_peer_body,
        "spread_peer",
        (channels // width,),
        [whole((half, block))] * 2 + [tile(block, width)],
        [tile(2 * half, width), whole((2 * half, block))],
        [struct((2 * half, channels), BF16), struct((2 * half, block), BF16)],
        4 * half * block * channels,
        2 * block * channels + 8 * half * block,
        scalars=1,
    )(core, mine, other, values)


def spread_own_body(row, values, piece):
    piece[...] = matmul(row[...], values[...]).astype(BF16)


def spread_own_call(row, values):
    share, block = row.shape
    channels = values.shape[1]
    width = min(channels, 512)
    return call(
        spread_own_body,
        "spread_own",
        (channels // width,),
        [whole((share, block)), tile(block, width)],
        tile(share, width),
        struct((share, channels), BF16),
        2 * share * block * channels,
        2 * block * channels + 2 * share * (block + channels),
    )(row, values)


def spread_gated_body(peers, tokens, halo, weight, cot, *refs):
    rows, pieces = refs[:peers], refs[peers:]
    conv, sig = gate_values(tokens, halo, weight)
    gated = (cot[...].astype(F32) * (conv * sig)).astype(BF16)
    for row, piece in zip(rows, pieces):
        piece[...] = matmul(row[...], gated).astype(BF16)


def spread_gated_call(tokens, halo, weight, cot, rows):
    block, channels = tokens.shape
    peers, share = len(rows), rows[0].shape[0]
    width = min(channels, 128)
    out = call(
        functools.partial(spread_gated_body, peers),
        "spread_gated",
        (channels // width,),
        [tile(block, width), tile(2, width), tile(3, width), tile(block, width)]
        + [whole((share, block))] * peers,
        [tile(share, width)] * peers,
        [struct((share, channels), BF16)] * peers,
        2 * peers * share * block * channels,
        4 * block * channels + 2 * peers * share * (block + channels),
        transcendentals=2 * block * channels,
    )(tokens, halo, weight, cot, *rows)
    return list(out)


def turn_body(peers, *refs):
    refs[peers][...] = join_rows(refs[:peers]).T


def turn_call(rows):
    share, block = rows[0].shape
    width = min(block, 256)
    return call(
        functools.partial(turn_body, len(rows)),
        "turn",
        (block // width,),
        [tile(share, width)] * len(rows),
        pl.BlockSpec((width, block), lambda c: (c, 0)),
        struct((block, block), BF16),
        block * block,
        4 * block * block,
    )(*rows)


def two_part(values):
    high = values.astype(BF16)
    return high, (values - high.astype(F32)).astype(BF16)


def middle_body(peers, span, with_grad, place, high, low, high_t, low_t, kern, *refs):
    pieces, refs = refs[:peers], refs[peers:]
    if with_grad:
        first, refs = refs[:peers], refs[peers:]
        grad, refs = refs[0], refs[1:]
    outs = refs[:peers]
    columns = pieces[0].shape[0]
    rows = [lax.bitwise_xor(place[0], r) for r in range(peers)]
    for g in range(columns // span):
        part = slice(g * span, (g + 1) * span)
        stacked = jnp.concatenate([piece[part] for piece in pieces], axis=0)
        mid = matmul(high[g], stacked) + matmul(low[g], stacked)
        if with_grad:
            stacked = jnp.concatenate([piece[part] for piece in first], axis=0)
            product = ((matmul(high[g], stacked) + matmul(low[g], stacked)) * mid).astype(BF16)
            for r in range(peers):
                grad[rows[r], part] = product[r * span : (r + 1) * span]
        filters = jnp.concatenate([kern[rows[r], part] for r in range(peers)], axis=0)
        upper, lower = two_part(filters.astype(F32) * mid)
        result = matmul(high_t[g], upper) + matmul(low_t[g], upper) + matmul(high_t[g], lower)
        result = result.astype(BF16)
        for r in range(peers):
            outs[r][part] = result[r * span : (r + 1) * span]


def middle_call(place, factors, kern, pieces, first=None):
    peers, columns, channels = kern.shape
    groups, side, _ = factors[0].shape
    width = min(channels, 256)
    cube = pl.BlockSpec((peers, columns, width), lambda c, *_: (0, 0, c))
    with_grad = first is not None
    n_in = peers * (2 if with_grad else 1)
    out = call(
        functools.partial(middle_body, peers, side // peers, with_grad),
        "middle_grad" if with_grad else "middle",
        (channels // width,),
        [whole((groups, side, side))] * 4 + [cube] + [tile(columns, width)] * n_in,
        ([cube] if with_grad else []) + [tile(columns, width)] * peers,
        ([struct(kern.shape, BF16)] if with_grad else []) + [struct((columns, channels), BF16)] * peers,
        (14 if with_grad else 10) * groups * side * side * channels,
        (10 if with_grad else 6) * peers * columns * channels + 8 * groups * side * side,
        scalars=1,
    )(place, *factors, kern, *pieces, *(first or []))
    return (out[0], list(out[1:])) if with_grad else list(out)


def middle_factors(outer, twiddle, place):
    peers, columns = twiddle.shape
    span = min(columns, max(16, 256 // peers))
    groups, side = columns // span, peers * span
    order = lax.bitwise_xor(jnp.arange(peers), place)
    pick = (order[:, None] == jnp.arange(peers)[None, :]).astype(F32)
    exact = functools.partial(jnp.dot, precision=lax.Precision.HIGHEST, preferred_element_type=F32)
    outer_here, twiddle_here = exact(exact(pick, outer), pick.T), exact(pick, twiddle)
    wide = jnp.repeat(jnp.repeat(outer_here, span, axis=0), span, axis=1)
    spot = jnp.arange(side) % span
    wide = jnp.where(spot[:, None] == spot[None, :], wide, 0.0)
    scale = twiddle_here.reshape(peers, groups, span).transpose(1, 0, 2).reshape(groups, 1, side)
    factor = wide[None] * scale
    high = lax.reduce_precision(factor, 8, 7)
    low = factor - high
    high, low = high.astype(BF16), low.astype(BF16)
    return high, low, high.transpose(0, 2, 1), low.transpose(0, 2, 1)


def join_rows(pieces):
    return jnp.concatenate([piece[...] for piece in pieces], axis=0)


def forward_body(peers, turned, weight, tokens, halo, cot, *refs):
    pieces, (mixed, back, head) = refs[:peers], refs[peers:]
    conv_out = matmul(turned[...], join_rows(pieces))
    conv, sig = gate_values(tokens, halo, weight)
    mixed[...] = (conv * sig * conv_out).astype(BF16)
    slope = sig * (1.0 + conv * (1.0 - sig))
    grad = cot[...].astype(F32) * conv_out * slope
    head[...] = grad[0:2]
    length = grad.shape[0]
    row = lax.broadcasted_iota(jnp.int32, grad.shape, 0)
    taps = weight[...]
    one_on = jnp.where(row < length - 1, pltpu.roll(grad, length - 1, 0), 0.0)
    two_on = jnp.where(row < length - 2, pltpu.roll(grad, length - 2, 0), 0.0)
    back[...] = taps[0:1] * grad + taps[1:2] * one_on + taps[2:3] * two_on


def forward_call(turned, weight, tokens, halo, cot, pieces):
    length, channels = tokens.shape
    peers, share = len(pieces), pieces[0].shape[0]
    width = min(channels, 128)
    return call(
        functools.partial(forward_body, peers),
        "forward_rows",
        (channels // width,),
        [whole(turned.shape), tile(3, width), tile(length, width), tile(2, width), tile(length, width)]
        + [tile(share, width)] * peers,
        [tile(length, width), tile(length, width), tile(2, width)],
        [struct((length, channels), BF16), struct((length, channels), F32), struct((2, channels), F32)],
        2 * length * length * channels,
        12 * length * channels + 2 * length * length,
        transcendentals=2 * length * channels,
    )(turned, weight, tokens, halo, cot, *pieces)


def in_vmem(count):
    return [pl.BlockSpec(memory_space=pltpu.VMEM)] * count


def partial_body(peers, width, turned, back, *refs):
    pieces, total = refs[:peers], refs[peers]
    depth = peers * pieces[0].shape[0]
    for c in range(total.shape[1] // width):
        part = slice(c * width, (c + 1) * width)
        stacked = jnp.concatenate([piece[:, part] for piece in pieces], axis=0)
        total[:, part] = matmul(turned[:, :depth], stacked) + back[:, part]


def partial_call(turned, back, pieces):
    length, channels = back.shape
    depth = len(pieces) * pieces[0].shape[0]
    return pl.pallas_call(
        functools.partial(partial_body, len(pieces), min(channels, 256)),
        name="backward_part",
        in_specs=in_vmem(2 + len(pieces)),
        out_specs=in_vmem(1)[0],
        out_shape=struct((length, channels), F32),
        compiler_params=pltpu.CompilerParams(vmem_limit_bytes=8 * MIB),
        cost_estimate=pl.CostEstimate(
            flops=2 * length * depth * channels, bytes_accessed=8 * length * channels, transcendentals=0
        ),
    )(turned, back, *pieces)


def backward_body(peers, width, turned, weight, back, tail, *refs):
    pieces, out, made, sems = refs[:peers], refs[peers], refs[peers + 1], refs[peers + 2]
    length, channels = made.shape
    depth = peers * pieces[0].shape[0]
    copies = []
    for c in range(channels // width):
        part = slice(c * width, (c + 1) * width)
        stacked = jnp.concatenate([piece[:, part] for piece in pieces], axis=0)
        total = matmul(turned[:, turned.shape[1] - depth :], stacked) + back[:, part]
        taps, edge = weight[:, part], tail[:, part]
        made[: length - 16, part] = total[: length - 16].astype(BF16)
        last = total[length - 16 :]
        row = lax.broadcasted_iota(jnp.int32, last.shape, 0)
        extra = jnp.where(row == 15, taps[1:2] * edge[0:1] + taps[2:3] * edge[1:2], 0.0)
        extra = jnp.where(row == 14, taps[2:3] * edge[0:1], extra)
        made[length - 16 :, part] = (last + extra).astype(BF16)
        copies.append(pltpu.make_async_copy(made.at[:, part], out.at[:, part], sems.at[c]))
        copies[-1].start()
    for copy in copies:
        copy.wait()


def backward_call(turned, weight, back, tail, pieces):
    length, channels = back.shape
    peers, depth = len(pieces), len(pieces) * pieces[0].shape[0]
    width = min(channels, 256)
    return pl.pallas_call(
        functools.partial(backward_body, peers, width),
        name="backward_rows",
        in_specs=in_vmem(4 + peers),
        out_specs=pl.BlockSpec(memory_space=pl.ANY),
        out_shape=struct((length, channels), BF16),
        scratch_shapes=[
            pltpu.VMEM((length, channels), BF16),
            pltpu.SemaphoreType.DMA((channels // width,)),
        ],
        compiler_params=pltpu.CompilerParams(vmem_limit_bytes=8 * MIB),
        cost_estimate=pl.CostEstimate(
            flops=2 * length * depth * channels, bytes_accessed=6 * length * channels, transcendentals=0
        ),
    )(turned, weight, back, tail, *pieces)


def after(value, *others):
    return lax.optimization_barrier((value, *others))[0]


class Wire:
    DEPTH = 5

    def __init__(self):
        self.ended = []

    def exchange(self, block, mask):
        if len(self.ended) >= self.DEPTH:
            block = after(block, self.ended[-self.DEPTH])
        self.ended.append(exchange(block, mask))
        return self.ended[-1]


def on_device(tokens, short_weight, inner_factor, outer_factor, twiddle, kernel, cotangent):
    peers = lax.axis_size("seq")
    place, core = lax.axis_index("seq"), lax.axis_index("ch")
    row_count, block, channels = tokens.shape
    assert row_count == 1 and lax.axis_size("ch") == 2
    flat, cot = tokens.reshape(block, channels), cotangent.reshape(block, channels)
    share = inner_factor.shape[0]
    place_ref, core_ref = place.reshape(1).astype(jnp.int32), core.reshape(1).astype(jnp.int32)
    assert peers & (peers - 1) == 0
    far = peers // 2
    others = [far] + [m for pair in zip(range(1, far), range(far + 1, peers)) for m in pair]
    arrival = [0] + others
    wire = Wire()

    half = lax.dynamic_slice(inner_factor, (core * (share // 2), 0), (share // 2, block))
    mine = {far: wire.exchange(half, far)}
    for m in range(1, far):
        mine[m] = wire.exchange(half, m)
    preceding = shifted(flat[-2:], 1)
    for m in range(1, far):
        mine[far + m] = wire.exchange(mine[far], m)

    rows, spread, pieces = {0: inner_factor}, {}, []
    for m in others:
        piece, rows[m] = spread_peer_call(core_ref, mine[m], swap_cores(mine[m]), flat)
        pieces.append(piece)
        spread[m] = wire.exchange(piece, m)
    held = after(flat, pieces[-1])
    spread[0] = spread_own_call(inner_factor, held)

    factors = middle_factors(outer_factor, twiddle, place)
    in_order = [rows[m] for m in range(peers)]
    spread_cot = spread_gated_call(held, preceding, short_weight, cot, in_order)
    spread_cot = {m: wire.exchange(spread_cot[m], m) for m in others} | {0: spread_cot[0]}
    turned = turn_call([rows[m] for m in arrival])

    spread = [spread[m] for m in range(peers)]
    mid = middle_call(place_ref, factors, kernel, spread)
    rows_fwd = {m: wire.exchange(mid[m], m) for m in others} | {0: mid[0]}
    spread_cot[0] = after(spread_cot[0], mid[0])
    kernel_grad, mid = middle_call(place_ref, factors, kernel, [spread_cot[m] for m in range(peers)], spread)
    rows_bwd = {0: mid[0]}
    for m in others[:-1]:
        rows_bwd[m] = wire.exchange(mid[m], m)
    rows_fwd[0] = after(rows_fwd[0], rows_bwd[others[0]])
    mixer_out, back, head = forward_call(
        turned, short_weight, flat, preceding, cot, [rows_fwd[m] for m in arrival]
    )
    following = shifted(head, -1)
    rows_bwd[others[-1]] = wire.exchange(after(mid[others[-1]], head), others[-1])
    late = max(1, peers // 4)
    back = partial_call(turned, back, [rows_bwd[m] for m in arrival[:-late]])
    token_grad = backward_call(turned, short_weight, back, following, [rows_bwd[m] for m in arrival[-late:]])
    return mixer_out.reshape(tokens.shape), token_grad.reshape(tokens.shape), kernel_grad


def solution(mesh):
    in_specs = (
        P(("grp", "seq"), None, "ch"),
        P(None, "ch"),
        P("seq", None),
        P(),
        P(None, "seq"),
        P(None, "seq", "ch"),
        P(("grp", "seq"), None, "ch"),
    )
    out_specs = (
        P(("grp", "seq"), None, "ch"),
        P(("grp", "seq"), None, "ch"),
        P("grp", "seq", "ch"),
    )
    return jax.shard_map(
        on_device, mesh=mesh, in_specs=in_specs, out_specs=out_specs, check_vma=False
    )
```

```python
import functools

import jax
import jax.numpy as jnp
from jax import lax
from jax.experimental import pallas as pl
from jax.experimental.pallas import tpu as pltpu
from jax.sharding import PartitionSpec as P

BF16, F32 = jnp.bfloat16, jnp.float32
MIB = 1024 * 1024
VMEM_LIMIT = 48 * MIB


def exchange(block, mask):
    return lax.ppermute(block, "seq", [(i, i ^ mask) for i in range(lax.axis_size("seq"))])


def shifted(block, distance):
    devices = range(lax.axis_size("seq"))
    return lax.ppermute(block, "seq", [(i - distance, i) for i in devices if i - distance in devices])


def swap_cores(block):
    return lax.ppermute(block, "ch", [(0, 1), (1, 0)])


def call(body, name, grid, in_specs, out_specs, out_shape, flops, moved, scalars=0, transcendentals=0):
    return pl.pallas_call(
        body,
        name=name,
        grid_spec=pltpu.PrefetchScalarGridSpec(
            num_scalar_prefetch=scalars, grid=grid, in_specs=in_specs, out_specs=out_specs
        ),
        out_shape=out_shape,
        compiler_params=pltpu.CompilerParams(vmem_limit_bytes=VMEM_LIMIT),
        cost_estimate=pl.CostEstimate(flops=flops, bytes_accessed=moved, transcendentals=transcendentals),
    )


def whole(shape):
    return pl.BlockSpec(shape, lambda c, *_: (0,) * len(shape))


def tile(rows, width):
    return pl.BlockSpec((rows, width), lambda c, *_: (0, c))


def struct(shape, dtype):
    return jax.ShapeDtypeStruct(shape, dtype)


def in_hbm(shape, dtype):
    return pltpu.HBM(shape, dtype)


def matmul(left, right):
    return jnp.dot(left, right, preferred_element_type=F32)


def gate_values(tokens, halo, weight):
    x = tokens[...].astype(F32)
    row = lax.broadcasted_iota(jnp.int32, x.shape, 0)
    edge, taps = halo[...].astype(F32), weight[...]
    one_back = jnp.where(row == 0, edge[1:2], pltpu.roll(x, 1, 0))
    two_back = jnp.where(row == 0, edge[0:1], jnp.where(row == 1, edge[1:2], pltpu.roll(x, 2, 0)))
    conv = taps[0:1] * x + taps[1:2] * one_back + taps[2:3] * two_back
    return conv, jax.nn.sigmoid(conv)


def spread_peer_body(core, mine, other, values, piece, rows):
    half = mine.shape[0]
    ours, theirs = matmul(mine[...], values[...]).astype(BF16), matmul(other[...], values[...]).astype(BF16)

    @pl.when(core[0] == 0)
    def _():
        piece[0:half], piece[half:] = ours, theirs
        rows[0:half], rows[half:] = mine[...], other[...]

    @pl.when(core[0] != 0)
    def _():
        piece[0:half], piece[half:] = theirs, ours
        rows[0:half], rows[half:] = other[...], mine[...]


def spread_peer_call(core, mine, other, values):
    half, block = mine.shape
    channels = values.shape[1]
    width = min(channels, 512)
    return call(
        spread_peer_body,
        "spread_peer",
        (channels // width,),
        [whole((half, block))] * 2 + [tile(block, width)],
        [tile(2 * half, width), whole((2 * half, block))],
        [struct((2 * half, channels), BF16), struct((2 * half, block), BF16)],
        4 * half * block * channels,
        2 * block * channels + 8 * half * block,
        scalars=1,
    )(core, mine, other, values)


def spread_own_body(row, values, piece):
    piece[...] = matmul(row[...], values[...]).astype(BF16)


def spread_own_call(row, values):
    share, block = row.shape
    channels = values.shape[1]
    width = min(channels, 512)
    return call(
        spread_own_body,
        "spread_own",
        (channels // width,),
        [whole((share, block)), tile(block, width)],
        tile(share, width),
        struct((share, channels), BF16),
        2 * share * block * channels,
        2 * block * channels + 2 * share * (block + channels),
    )(row, values)


def spread_gated_body(peers, tokens, halo, weight, cot, *refs):
    rows, pieces = refs[:peers], refs[peers:]
    conv, sig = gate_values(tokens, halo, weight)
    gated = (cot[...].astype(F32) * (conv * sig)).astype(BF16)
    for row, piece in zip(rows, pieces):
        piece[...] = matmul(row[...], gated).astype(BF16)


def spread_gated_call(tokens, halo, weight, cot, rows):
    block, channels = tokens.shape
    peers, share = len(rows), rows[0].shape[0]
    width = min(channels, 128)
    out = call(
        functools.partial(spread_gated_body, peers),
        "spread_gated",
        (channels // width,),
        [tile(block, width), tile(2, width), tile(3, width), tile(block, width)]
        + [whole((share, block))] * peers,
        [tile(share, width)] * peers,
        [in_hbm((share, channels), BF16)] * peers,
        2 * peers * share * block * channels,
        4 * block * channels + 2 * peers * share * (block + channels),
        transcendentals=2 * block * channels,
    )(tokens, halo, weight, cot, *rows)
    return list(out)


def turn_body(peers, *refs):
    refs[peers][...] = join_rows(refs[:peers]).T


def turn_call(rows):
    share, block = rows[0].shape
    width = min(block, 256)
    return call(
        functools.partial(turn_body, len(rows)),
        "turn",
        (block // width,),
        [tile(share, width)] * len(rows),
        pl.BlockSpec((width, block), lambda c: (c, 0)),
        struct((block, block), BF16),
        block * block,
        4 * block * block,
    )(*rows)


def two_part(values):
    high = values.astype(BF16)
    return high, (values - high.astype(F32)).astype(BF16)


def middle_body(peers, span, with_grad, place, high, low, high_t, low_t, kern, *refs):
    pieces, refs = refs[:peers], refs[peers:]
    if with_grad:
        first, refs = refs[:peers], refs[peers:]
        grad, refs = refs[0], refs[1:]
    outs = refs[:peers]
    columns = pieces[0].shape[0]
    rows = [lax.bitwise_xor(place[0], r) for r in range(peers)]
    for g in range(columns // span):
        part = slice(g * span, (g + 1) * span)
        stacked = jnp.concatenate([piece[part] for piece in pieces], axis=0)
        mid = matmul(high[g], stacked) + matmul(low[g], stacked)
        if with_grad:
            stacked = jnp.concatenate([piece[part] for piece in first], axis=0)
            product = ((matmul(high[g], stacked) + matmul(low[g], stacked)) * mid).astype(BF16)
            for r in range(peers):
                grad[rows[r], part] = product[r * span : (r + 1) * span]
        filters = jnp.concatenate([kern[rows[r], part] for r in range(peers)], axis=0)
        upper, lower = two_part(filters.astype(F32) * mid)
        result = matmul(high_t[g], upper) + matmul(low_t[g], upper) + matmul(high_t[g], lower)
        result = result.astype(BF16)
        for r in range(peers):
            outs[r][part] = result[r * span : (r + 1) * span]


def middle_call(place, factors, kern, pieces, first=None):
    peers, columns, channels = kern.shape
    groups, side, _ = factors[0].shape
    width = min(channels, 256)
    cube = pl.BlockSpec((peers, columns, width), lambda c, *_: (0, 0, c))
    with_grad = first is not None
    n_in = peers * (2 if with_grad else 1)
    out = call(
        functools.partial(middle_body, peers, side // peers, with_grad),
        "middle_grad" if with_grad else "middle",
        (channels // width,),
        [whole((groups, side, side))] * 4 + [cube] + [tile(columns, width)] * n_in,
        ([cube] if with_grad else []) + [tile(columns, width)] * peers,
        ([struct(kern.shape, BF16)] if with_grad else []) + [in_hbm((columns, channels), BF16)] * peers,
        (14 if with_grad else 10) * groups * side * side * channels,
        (10 if with_grad else 6) * peers * columns * channels + 8 * groups * side * side,
        scalars=1,
    )(place, *factors, kern, *pieces, *(first or []))
    return (out[0], list(out[1:])) if with_grad else list(out)


def exact(left, right):
    return jnp.dot(left, right, precision=lax.Precision.HIGHEST, preferred_element_type=F32)


def factors_body(span, place, outer, twiddle, high, low, high_t, low_t):
    peers, columns = twiddle.shape
    side = peers * span

    def spots(shape, axis):
        return lax.broadcasted_iota(jnp.int32, shape, axis)

    pick = jnp.where(lax.bitwise_xor(spots((peers, peers), 0), place[0]) == spots((peers, peers), 1), 1.0, 0.0)
    spread_rows = jnp.where(lax.div(spots((side, peers), 0), span) == spots((side, peers), 1), 1.0, 0.0)
    owner = lax.div(spots((peers, side), 1), span) == spots((peers, side), 0)
    spread_columns = jnp.where(owner, 1.0, 0.0)
    outer_here = exact(pick, exact(outer[...], pick))
    twiddle_here = exact(pick, twiddle[...])
    wide = exact(exact(spread_rows, outer_here), spread_columns)
    same = lax.rem(spots((side, side), 0), span) == lax.rem(spots((side, side), 1), span)
    wide = jnp.where(same, wide, 0.0)
    for g in range(columns // span):
        at = lax.rem(spots((columns, side), 1), span) + g * span == spots((columns, side), 0)
        scale = exact(twiddle_here, jnp.where(at, 1.0, 0.0))
        scale = jnp.sum(jnp.where(owner, scale, 0.0), axis=0, keepdims=True)
        factor = wide * scale
        high[g], low[g] = two_part(factor)
        high_t[g], low_t[g] = two_part(factor.T)


def middle_factors(outer, twiddle, place):
    peers, columns = twiddle.shape
    span = min(columns, max(16, 256 // peers))
    groups, side = columns // span, peers * span
    shape = (groups, side, side)
    return call(
        functools.partial(factors_body, span),
        "factors",
        (1,),
        [whole(outer.shape), whole(twiddle.shape)],
        [whole(shape)] * 4,
        [struct(shape, BF16)] * 4,
        16 * groups * side * side,
        8 * groups * side * side,
        scalars=1,
    )(place, outer, twiddle)


def join_rows(pieces):
    return jnp.concatenate([piece[...] for piece in pieces], axis=0)


def forward_body(peers, turned, weight, tokens, halo, cot, *refs):
    pieces, (mixed, back, head) = refs[:peers], refs[peers:]
    conv_out = matmul(turned[...], join_rows(pieces))
    conv, sig = gate_values(tokens, halo, weight)
    mixed[...] = (conv * sig * conv_out).astype(BF16)
    slope = sig * (1.0 + conv * (1.0 - sig))
    grad = cot[...].astype(F32) * conv_out * slope
    head[...] = grad[0:2]
    length = grad.shape[0]
    row = lax.broadcasted_iota(jnp.int32, grad.shape, 0)
    taps = weight[...]
    one_on = jnp.where(row < length - 1, pltpu.roll(grad, length - 1, 0), 0.0)
    two_on = jnp.where(row < length - 2, pltpu.roll(grad, length - 2, 0), 0.0)
    back[...] = taps[0:1] * grad + taps[1:2] * one_on + taps[2:3] * two_on


def forward_call(turned, weight, tokens, halo, cot, pieces):
    length, channels = tokens.shape
    peers, share = len(pieces), pieces[0].shape[0]
    width = min(channels, 128)
    return call(
        functools.partial(forward_body, peers),
        "forward_rows",
        (channels // width,),
        [whole(turned.shape), tile(3, width), tile(length, width), tile(2, width), tile(length, width)]
        + [tile(share, width)] * peers,
        [tile(length, width), tile(length, width), tile(2, width)],
        [struct((length, channels), BF16), struct((length, channels), F32), struct((2, channels), F32)],
        2 * length * length * channels,
        12 * length * channels + 2 * length * length,
        transcendentals=2 * length * channels,
    )(turned, weight, tokens, halo, cot, *pieces)


def in_vmem(count):
    return [pl.BlockSpec(memory_space=pltpu.VMEM)] * count


def partial_body(peers, width, turned, back, *refs):
    pieces, total = refs[:peers], refs[peers]
    depth = peers * pieces[0].shape[0]
    for c in range(total.shape[1] // width):
        part = slice(c * width, (c + 1) * width)
        stacked = jnp.concatenate([piece[:, part] for piece in pieces], axis=0)
        total[:, part] = matmul(turned[:, :depth], stacked) + back[:, part]


def partial_call(turned, back, pieces):
    length, channels = back.shape
    depth = len(pieces) * pieces[0].shape[0]
    return pl.pallas_call(
        functools.partial(partial_body, len(pieces), min(channels, 256)),
        name="backward_part",
        in_specs=in_vmem(2 + len(pieces)),
        out_specs=in_vmem(1)[0],
        out_shape=struct((length, channels), F32),
        compiler_params=pltpu.CompilerParams(vmem_limit_bytes=8 * MIB),
        cost_estimate=pl.CostEstimate(
            flops=2 * length * depth * channels, bytes_accessed=8 * length * channels, transcendentals=0
        ),
    )(turned, back, *pieces)


def backward_body(peers, width, turned, weight, back, tail, *refs):
    pieces, out, made, sems = refs[:peers], refs[peers], refs[peers + 1], refs[peers + 2]
    length, channels = made.shape
    depth = peers * pieces[0].shape[0]
    copies = []
    for c in range(channels // width):
        part = slice(c * width, (c + 1) * width)
        stacked = jnp.concatenate([piece[:, part] for piece in pieces], axis=0)
        total = matmul(turned[:, turned.shape[1] - depth :], stacked) + back[:, part]
        taps, edge = weight[:, part], tail[:, part]
        made[: length - 16, part] = total[: length - 16].astype(BF16)
        last = total[length - 16 :]
        row = lax.broadcasted_iota(jnp.int32, last.shape, 0)
        extra = jnp.where(row == 15, taps[1:2] * edge[0:1] + taps[2:3] * edge[1:2], 0.0)
        extra = jnp.where(row == 14, taps[2:3] * edge[0:1], extra)
        made[length - 16 :, part] = (last + extra).astype(BF16)
        copies.append(pltpu.make_async_copy(made.at[:, part], out.at[:, part], sems.at[c]))
        copies[-1].start()
    for copy in copies:
        copy.wait()


def backward_call(turned, weight, back, tail, pieces):
    length, channels = back.shape
    peers, depth = len(pieces), len(pieces) * pieces[0].shape[0]
    width = min(channels, 256)
    return pl.pallas_call(
        functools.partial(backward_body, peers, width),
        name="backward_rows",
        in_specs=in_vmem(4 + peers),
        out_specs=pl.BlockSpec(memory_space=pl.ANY),
        out_shape=struct((length, channels), BF16),
        scratch_shapes=[
            pltpu.VMEM((length, channels), BF16),
            pltpu.SemaphoreType.DMA((channels // width,)),
        ],
        compiler_params=pltpu.CompilerParams(vmem_limit_bytes=8 * MIB),
        cost_estimate=pl.CostEstimate(
            flops=2 * length * depth * channels, bytes_accessed=6 * length * channels, transcendentals=0
        ),
    )(turned, weight, back, tail, *pieces)


def after(value, *others):
    return lax.optimization_barrier((value, *others))[0]


class Wire:
    DEPTH = 5

    def __init__(self):
        self.ended = []

    def exchange(self, block, mask):
        if len(self.ended) >= self.DEPTH:
            block = after(block, self.ended[-self.DEPTH])
        self.ended.append(exchange(block, mask))
        return self.ended[-1]


def on_device(tokens, short_weight, inner_factor, outer_factor, twiddle, kernel, cotangent):
    peers = lax.axis_size("seq")
    place, core = lax.axis_index("seq"), lax.axis_index("ch")
    row_count, block, channels = tokens.shape
    assert row_count == 1 and lax.axis_size("ch") == 2
    flat, cot = tokens.reshape(block, channels), cotangent.reshape(block, channels)
    share = inner_factor.shape[0]
    place_ref, core_ref = place.reshape(1).astype(jnp.int32), core.reshape(1).astype(jnp.int32)
    assert peers & (peers - 1) == 0
    far = peers // 2
    others = [far] + [m for pair in zip(range(1, far), range(far + 1, peers)) for m in pair]
    arrival = [0] + others
    wire = Wire()

    half = lax.dynamic_slice(inner_factor, (core * (share // 2), 0), (share // 2, block))
    mine = {far: wire.exchange(half, far)}
    for m in range(1, far):
        mine[m] = wire.exchange(half, m)
    preceding = shifted(flat[-2:], 1)
    for m in range(1, far):
        mine[far + m] = wire.exchange(mine[far], m)

    rows, spread, pieces = {0: inner_factor}, {}, []
    for m in others:
        piece, rows[m] = spread_peer_call(core_ref, mine[m], swap_cores(mine[m]), flat)
        pieces.append(piece)
        spread[m] = wire.exchange(piece, m)
    held = after(flat, pieces[-1])
    spread[0] = spread_own_call(inner_factor, held)

    in_order = [rows[m] for m in range(peers)]
    spread_cot = spread_gated_call(held, preceding, short_weight, cot, in_order)
    factors = middle_factors(after(outer_factor, spread_cot[0]), twiddle, place_ref)
    spread_cot = {m: wire.exchange(spread_cot[m], m) for m in others} | {0: spread_cot[0]}
    turned = turn_call([rows[m] for m in arrival])

    spread = [spread[m] for m in range(peers)]
    mid = middle_call(place_ref, factors, kernel, spread)
    rows_fwd = {m: wire.exchange(mid[m], m) for m in others} | {0: mid[0]}
    spread_cot[0] = after(spread_cot[0], mid[0])
    kernel_grad, mid = middle_call(place_ref, factors, kernel, [spread_cot[m] for m in range(peers)], spread)
    rows_bwd = {0: mid[0]}
    for m in others[:-2]:
        rows_bwd[m] = wire.exchange(mid[m], m)
    mixer_out, back, head = forward_call(
        turned, short_weight, flat, preceding, cot, [rows_fwd[m] for m in arrival]
    )
    following = shifted(head, -1)
    for m in others[-2:]:
        rows_bwd[m] = wire.exchange(after(mid[m], head), m)
    late = max(1, peers // 4)
    back = partial_call(turned, back, [rows_bwd[m] for m in arrival[:-late]])
    token_grad = backward_call(turned, short_weight, back, following, [rows_bwd[m] for m in arrival[-late:]])
    return mixer_out.reshape(tokens.shape), token_grad.reshape(tokens.shape), kernel_grad


def solution(mesh):
    in_specs = (
        P(("grp", "seq"), None, "ch"),
        P(None, "ch"),
        P("seq", None),
        P(),
        P(None, "seq"),
        P(None, "seq", "ch"),
        P(("grp", "seq"), None, "ch"),
    )
    out_specs = (
        P(("grp", "seq"), None, "ch"),
        P(("grp", "seq"), None, "ch"),
        P("grp", "seq", "ch"),
    )
    return jax.shard_map(
        on_device, mesh=mesh, in_specs=in_specs, out_specs=out_specs, check_vma=False
    )
```

```python
import functools

import jax
import jax.numpy as jnp
from jax import lax
from jax.experimental import pallas as pl
from jax.experimental.pallas import tpu as pltpu
from jax.sharding import PartitionSpec as P

BF16, F32 = jnp.bfloat16, jnp.float32
MIB = 1024 * 1024
VMEM_LIMIT = 48 * MIB


def exchange(block, mask):
    return lax.ppermute(block, "seq", [(i, i ^ mask) for i in range(lax.axis_size("seq"))])


def shifted(block, distance):
    devices = range(lax.axis_size("seq"))
    return lax.ppermute(block, "seq", [(i - distance, i) for i in devices if i - distance in devices])


def swap_cores(block):
    return lax.ppermute(block, "ch", [(0, 1), (1, 0)])


def call(body, name, grid, in_specs, out_specs, out_shape, flops, moved, scalars=0, transcendentals=0):
    return pl.pallas_call(
        body,
        name=name,
        grid_spec=pltpu.PrefetchScalarGridSpec(
            num_scalar_prefetch=scalars, grid=grid, in_specs=in_specs, out_specs=out_specs
        ),
        out_shape=out_shape,
        compiler_params=pltpu.CompilerParams(vmem_limit_bytes=VMEM_LIMIT),
        cost_estimate=pl.CostEstimate(flops=flops, bytes_accessed=moved, transcendentals=transcendentals),
    )


def whole(shape):
    return pl.BlockSpec(shape, lambda c, *_: (0,) * len(shape))


def tile(rows, width):
    return pl.BlockSpec((rows, width), lambda c, *_: (0, c))


def struct(shape, dtype):
    return jax.ShapeDtypeStruct(shape, dtype)


def in_hbm(shape, dtype):
    return pltpu.HBM(shape, dtype)


def matmul(left, right):
    return jnp.dot(left, right, preferred_element_type=F32)


def gate_values(tokens, halo, weight):
    x = tokens[...].astype(F32)
    row = lax.broadcasted_iota(jnp.int32, x.shape, 0)
    edge, taps = halo[...].astype(F32), weight[...]
    one_back = jnp.where(row == 0, edge[1:2], pltpu.roll(x, 1, 0))
    two_back = jnp.where(row == 0, edge[0:1], jnp.where(row == 1, edge[1:2], pltpu.roll(x, 2, 0)))
    conv = taps[0:1] * x + taps[1:2] * one_back + taps[2:3] * two_back
    return conv, jax.nn.sigmoid(conv)


def spread_peer_body(core, mine, other, values, piece, rows):
    half = mine.shape[0]
    ours, theirs = matmul(mine[...], values[...]).astype(BF16), matmul(other[...], values[...]).astype(BF16)

    @pl.when(core[0] == 0)
    def _():
        piece[0:half], piece[half:] = ours, theirs
        rows[0:half], rows[half:] = mine[...], other[...]

    @pl.when(core[0] != 0)
    def _():
        piece[0:half], piece[half:] = theirs, ours
        rows[0:half], rows[half:] = other[...], mine[...]


def spread_peer_call(core, mine, other, values):
    half, block = mine.shape
    channels = values.shape[1]
    width = channels
    return call(
        spread_peer_body,
        "spread_peer",
        (channels // width,),
        [whole((half, block))] * 2 + [tile(block, width)],
        [tile(2 * half, width), whole((2 * half, block))],
        [struct((2 * half, channels), BF16), struct((2 * half, block), BF16)],
        4 * half * block * channels,
        2 * block * channels + 8 * half * block,
        scalars=1,
    )(core, mine, other, values)


def spread_own_body(row, values, piece):
    piece[...] = matmul(row[...], values[...]).astype(BF16)


def spread_own_call(row, values):
    share, block = row.shape
    channels = values.shape[1]
    width = min(channels, 512)
    return call(
        spread_own_body,
        "spread_own",
        (channels // width,),
        [whole((share, block)), tile(block, width)],
        tile(share, width),
        struct((share, channels), BF16),
        2 * share * block * channels,
        2 * block * channels + 2 * share * (block + channels),
    )(row, values)


def spread_gated_body(peers, tokens, halo, weight, cot, *refs):
    rows, pieces = refs[:peers], refs[peers:]
    conv, sig = gate_values(tokens, halo, weight)
    gated = (cot[...].astype(F32) * (conv * sig)).astype(BF16)
    for row, piece in zip(rows, pieces):
        piece[...] = matmul(row[...], gated).astype(BF16)


def spread_gated_call(tokens, halo, weight, cot, rows):
    block, channels = tokens.shape
    peers, share = len(rows), rows[0].shape[0]
    width = min(channels, 128)
    out = call(
        functools.partial(spread_gated_body, peers),
        "spread_gated",
        (channels // width,),
        [tile(block, width), tile(2, width), tile(3, width), tile(block, width)]
        + [whole((share, block))] * peers,
        [tile(share, width)] * peers,
        [in_hbm((share, channels), BF16)] * peers,
        2 * peers * share * block * channels,
        4 * block * channels + 2 * peers * share * (block + channels),
        transcendentals=2 * block * channels,
    )(tokens, halo, weight, cot, *rows)
    return list(out)


def turn_body(peers, *refs):
    refs[peers][...] = join_rows(refs[:peers]).T


def turn_call(rows):
    share, block = rows[0].shape
    width = min(block, 256)
    return call(
        functools.partial(turn_body, len(rows)),
        "turn",
        (block // width,),
        [tile(share, width)] * len(rows),
        pl.BlockSpec((width, block), lambda c: (c, 0)),
        struct((block, block), BF16),
        block * block,
        4 * block * block,
    )(*rows)


def two_part(values):
    high = values.astype(BF16)
    return high, (values - high.astype(F32)).astype(BF16)


def middle_body(peers, span, with_grad, place, high, low, high_t, low_t, kern, *refs):
    pieces, refs = refs[:peers], refs[peers:]
    if with_grad:
        first, refs = refs[:peers], refs[peers:]
        grad, refs = refs[0], refs[1:]
    outs = refs[:peers]
    columns = pieces[0].shape[0]
    rows = [lax.bitwise_xor(place[0], r) for r in range(peers)]
    for g in range(columns // span):
        part = slice(g * span, (g + 1) * span)
        stacked = jnp.concatenate([piece[part] for piece in pieces], axis=0)
        mid = matmul(high[g], stacked) + matmul(low[g], stacked)
        if with_grad:
            stacked = jnp.concatenate([piece[part] for piece in first], axis=0)
            product = ((matmul(high[g], stacked) + matmul(low[g], stacked)) * mid).astype(BF16)
            for r in range(peers):
                grad[rows[r], part] = product[r * span : (r + 1) * span]
        filters = jnp.concatenate([kern[rows[r], part] for r in range(peers)], axis=0)
        upper, lower = two_part(filters.astype(F32) * mid)
        result = matmul(high_t[g], upper) + matmul(low_t[g], upper) + matmul(high_t[g], lower)
        result = result.astype(BF16)
        for r in range(peers):
            outs[r][part] = result[r * span : (r + 1) * span]


def middle_call(place, factors, kern, pieces, first=None):
    peers, columns, channels = kern.shape
    groups, side, _ = factors[0].shape
    width = min(channels, 256)
    cube = pl.BlockSpec((peers, columns, width), lambda c, *_: (0, 0, c))
    with_grad = first is not None
    n_in = peers * (2 if with_grad else 1)
    out = call(
        functools.partial(middle_body, peers, side // peers, with_grad),
        "middle_grad" if with_grad else "middle",
        (channels // width,),
        [whole((groups, side, side))] * 4 + [cube] + [tile(columns, width)] * n_in,
        ([cube] if with_grad else []) + [tile(columns, width)] * peers,
        ([struct(kern.shape, BF16)] if with_grad else []) + [in_hbm((columns, channels), BF16)] * peers,
        (14 if with_grad else 10) * groups * side * side * channels,
        (10 if with_grad else 6) * peers * columns * channels + 8 * groups * side * side,
        scalars=1,
    )(place, *factors, kern, *pieces, *(first or []))
    return (out[0], list(out[1:])) if with_grad else list(out)


def exact(left, right):
    return jnp.dot(left, right, precision=lax.Precision.HIGHEST, preferred_element_type=F32)


def factors_body(span, place, outer, twiddle, high, low, high_t, low_t):
    peers, columns = twiddle.shape
    side = peers * span

    def spots(shape, axis):
        return lax.broadcasted_iota(jnp.int32, shape, axis)

    pick = jnp.where(lax.bitwise_xor(spots((peers, peers), 0), place[0]) == spots((peers, peers), 1), 1.0, 0.0)
    spread_rows = jnp.where(lax.div(spots((side, peers), 0), span) == spots((side, peers), 1), 1.0, 0.0)
    owner = lax.div(spots((peers, side), 1), span) == spots((peers, side), 0)
    spread_columns = jnp.where(owner, 1.0, 0.0)
    outer_here = exact(pick, exact(outer[...], pick))
    twiddle_here = exact(pick, twiddle[...])
    wide = exact(exact(spread_rows, outer_here), spread_columns)
    same = lax.rem(spots((side, side), 0), span) == lax.rem(spots((side, side), 1), span)
    wide = jnp.where(same, wide, 0.0)
    for g in range(columns // span):
        at = lax.rem(spots((columns, side), 1), span) + g * span == spots((columns, side), 0)
        scale = exact(twiddle_here, jnp.where(at, 1.0, 0.0))
        scale = jnp.sum(jnp.where(owner, scale, 0.0), axis=0, keepdims=True)
        factor = wide * scale
        high[g], low[g] = two_part(factor)
        high_t[g], low_t[g] = two_part(factor.T)


def middle_factors(outer, twiddle, place):
    peers, columns = twiddle.shape
    span = min(columns, max(16, 256 // peers))
    groups, side = columns // span, peers * span
    shape = (groups, side, side)
    return call(
        functools.partial(factors_body, span),
        "factors",
        (1,),
        [whole(outer.shape), whole(twiddle.shape)],
        [whole(shape)] * 4,
        [struct(shape, BF16)] * 4,
        16 * groups * side * side,
        8 * groups * side * side,
        scalars=1,
    )(place, outer, twiddle)


def join_rows(pieces):
    return jnp.concatenate([piece[...] for piece in pieces], axis=0)


def forward_body(peers, turned, weight, tokens, halo, cot, *refs):
    pieces, (mixed, back, head) = refs[:peers], refs[peers:]
    conv_out = matmul(turned[...], join_rows(pieces))
    conv, sig = gate_values(tokens, halo, weight)
    mixed[...] = (conv * sig * conv_out).astype(BF16)
    slope = sig * (1.0 + conv * (1.0 - sig))
    grad = cot[...].astype(F32) * conv_out * slope
    head[...] = grad[0:2]
    length = grad.shape[0]
    row = lax.broadcasted_iota(jnp.int32, grad.shape, 0)
    taps = weight[...]
    one_on = jnp.where(row < length - 1, pltpu.roll(grad, length - 1, 0), 0.0)
    two_on = jnp.where(row < length - 2, pltpu.roll(grad, length - 2, 0), 0.0)
    back[...] = taps[0:1] * grad + taps[1:2] * one_on + taps[2:3] * two_on


def forward_call(turned, weight, tokens, halo, cot, pieces):
    length, channels = tokens.shape
    peers, share = len(pieces), pieces[0].shape[0]
    width = min(channels, 128)
    return call(
        functools.partial(forward_body, peers),
        "forward_rows",
        (channels // width,),
        [whole(turned.shape), tile(3, width), tile(length, width), tile(2, width), tile(length, width)]
        + [tile(share, width)] * peers,
        [tile(length, width), tile(length, width), tile(2, width)],
        [struct((length, channels), BF16), struct((length, channels), F32), struct((2, channels), F32)],
        2 * length * length * channels,
        12 * length * channels + 2 * length * length,
        transcendentals=2 * length * channels,
    )(turned, weight, tokens, halo, cot, *pieces)


def in_vmem(count):
    return [pl.BlockSpec(memory_space=pltpu.VMEM)] * count


def partial_body(peers, width, turned, back, *refs):
    pieces, total = refs[:peers], refs[peers]
    depth = peers * pieces[0].shape[0]
    for c in range(total.shape[1] // width):
        part = slice(c * width, (c + 1) * width)
        stacked = jnp.concatenate([piece[:, part] for piece in pieces], axis=0)
        total[:, part] = matmul(turned[:, :depth], stacked) + back[:, part]


def partial_call(turned, back, pieces):
    length, channels = back.shape
    depth = len(pieces) * pieces[0].shape[0]
    return pl.pallas_call(
        functools.partial(partial_body, len(pieces), min(channels, 256)),
        name="backward_part",
        in_specs=in_vmem(2 + len(pieces)),
        out_specs=in_vmem(1)[0],
        out_shape=struct((length, channels), F32),
        compiler_params=pltpu.CompilerParams(vmem_limit_bytes=8 * MIB),
        cost_estimate=pl.CostEstimate(
            flops=2 * length * depth * channels, bytes_accessed=8 * length * channels, transcendentals=0
        ),
    )(turned, back, *pieces)


def backward_body(peers, width, turned, weight, back, tail, *refs):
    pieces, out, made, sems = refs[:peers], refs[peers], refs[peers + 1], refs[peers + 2]
    length, channels = made.shape
    depth = peers * pieces[0].shape[0]
    copies = []
    for c in range(channels // width):
        part = slice(c * width, (c + 1) * width)
        stacked = jnp.concatenate([piece[:, part] for piece in pieces], axis=0)
        total = matmul(turned[:, turned.shape[1] - depth :], stacked) + back[:, part]
        taps, edge = weight[:, part], tail[:, part]
        made[: length - 16, part] = total[: length - 16].astype(BF16)
        last = total[length - 16 :]
        row = lax.broadcasted_iota(jnp.int32, last.shape, 0)
        extra = jnp.where(row == 15, taps[1:2] * edge[0:1] + taps[2:3] * edge[1:2], 0.0)
        extra = jnp.where(row == 14, taps[2:3] * edge[0:1], extra)
        made[length - 16 :, part] = (last + extra).astype(BF16)
        copies.append(pltpu.make_async_copy(made.at[:, part], out.at[:, part], sems.at[c]))
        copies[-1].start()
    for copy in copies:
        copy.wait()


def backward_call(turned, weight, back, tail, pieces):
    length, channels = back.shape
    peers, depth = len(pieces), len(pieces) * pieces[0].shape[0]
    width = min(channels, 256)
    return pl.pallas_call(
        functools.partial(backward_body, peers, width),
        name="backward_rows",
        in_specs=in_vmem(4 + peers),
        out_specs=pl.BlockSpec(memory_space=pl.ANY),
        out_shape=struct((length, channels), BF16),
        scratch_shapes=[
            pltpu.VMEM((length, channels), BF16),
            pltpu.SemaphoreType.DMA((channels // width,)),
        ],
        compiler_params=pltpu.CompilerParams(vmem_limit_bytes=8 * MIB),
        cost_estimate=pl.CostEstimate(
            flops=2 * length * depth * channels, bytes_accessed=6 * length * channels, transcendentals=0
        ),
    )(turned, weight, back, tail, *pieces)


def after(value, *others):
    return lax.optimization_barrier((value, *others))[0]


class Wire:
    DEPTH = 5

    def __init__(self):
        self.ended = []

    def exchange(self, block, mask):
        if len(self.ended) >= self.DEPTH:
            block = after(block, self.ended[-self.DEPTH])
        self.ended.append(exchange(block, mask))
        return self.ended[-1]


def on_device(tokens, short_weight, inner_factor, outer_factor, twiddle, kernel, cotangent):
    peers = lax.axis_size("seq")
    place, core = lax.axis_index("seq"), lax.axis_index("ch")
    row_count, block, channels = tokens.shape
    assert row_count == 1 and lax.axis_size("ch") == 2
    flat, cot = tokens.reshape(block, channels), cotangent.reshape(block, channels)
    share = inner_factor.shape[0]
    place_ref, core_ref = place.reshape(1).astype(jnp.int32), core.reshape(1).astype(jnp.int32)
    assert peers & (peers - 1) == 0
    far = peers // 2
    others = [far] + [m for pair in zip(range(1, far), range(far + 1, peers)) for m in pair]
    arrival = [0] + others
    wire = Wire()

    half = lax.dynamic_slice(inner_factor, (core * (share // 2), 0), (share // 2, block))
    mine = {far: wire.exchange(half, far)}
    for m in range(1, far):
        mine[m] = wire.exchange(half, m)
    preceding = shifted(flat[-2:], 1)
    for m in range(1, far):
        mine[far + m] = wire.exchange(mine[far], m)

    rows, spread, pieces = {0: inner_factor}, {}, []
    for m in others:
        piece, rows[m] = spread_peer_call(core_ref, mine[m], swap_cores(mine[m]), flat)
        pieces.append(piece)
        spread[m] = wire.exchange(piece, m)
    held = after(flat, pieces[-1])
    spread[0] = spread_own_call(inner_factor, held)

    in_order = [rows[m] for m in range(peers)]
    spread_cot = spread_gated_call(held, preceding, short_weight, cot, in_order)
    factors = middle_factors(after(outer_factor, spread_cot[0]), twiddle, place_ref)
    spread_cot = {m: wire.exchange(spread_cot[m], m) for m in others} | {0: spread_cot[0]}
    turned = turn_call([rows[m] for m in arrival])

    spread = [spread[m] for m in range(peers)]
    mid = middle_call(place_ref, factors, kernel, spread)
    rows_fwd = {m: wire.exchange(mid[m], m) for m in others} | {0: mid[0]}
    spread_cot[0] = after(spread_cot[0], mid[0])
    kernel_grad, mid = middle_call(place_ref, factors, kernel, [spread_cot[m] for m in range(peers)], spread)
    rows_bwd = {0: mid[0]}
    for m in others[:-2]:
        rows_bwd[m] = wire.exchange(mid[m], m)
    mixer_out, back, head = forward_call(
        turned, short_weight, flat, preceding, cot, [rows_fwd[m] for m in arrival]
    )
    following = shifted(head, -1)
    for m in others[-2:]:
        rows_bwd[m] = wire.exchange(after(mid[m], head), m)
    late = max(1, peers // 4)
    back = partial_call(turned, back, [rows_bwd[m] for m in arrival[:-late]])
    token_grad = backward_call(turned, short_weight, back, following, [rows_bwd[m] for m in arrival[-late:]])
    return mixer_out.reshape(tokens.shape), token_grad.reshape(tokens.shape), kernel_grad


def solution(mesh):
    in_specs = (
        P(("grp", "seq"), None, "ch"),
        P(None, "ch"),
        P("seq", None),
        P(),
        P(None, "seq"),
        P(None, "seq", "ch"),
        P(("grp", "seq"), None, "ch"),
    )
    out_specs = (
        P(("grp", "seq"), None, "ch"),
        P(("grp", "seq"), None, "ch"),
        P("grp", "seq", "ch"),
    )
    return jax.shard_map(
        on_device, mesh=mesh, in_specs=in_specs, out_specs=out_specs, check_vma=False
    )
```

```python
import functools

import jax
import jax.numpy as jnp
from jax import lax
from jax.experimental import pallas as pl
from jax.experimental.pallas import tpu as pltpu
from jax.sharding import PartitionSpec as P

BF16, F32 = jnp.bfloat16, jnp.float32
MIB = 1024 * 1024
VMEM_LIMIT = 48 * MIB


def exchange(block, mask):
    return lax.ppermute(block, "seq", [(i, i ^ mask) for i in range(lax.axis_size("seq"))])


def shifted(block, distance):
    devices = range(lax.axis_size("seq"))
    return lax.ppermute(block, "seq", [(i - distance, i) for i in devices if i - distance in devices])


def swap_cores(block):
    return lax.ppermute(block, "ch", [(0, 1), (1, 0)])


def call(body, name, grid, in_specs, out_specs, out_shape, flops, moved, scalars=0, transcendentals=0):
    return pl.pallas_call(
        body,
        name=name,
        grid_spec=pltpu.PrefetchScalarGridSpec(
            num_scalar_prefetch=scalars, grid=grid, in_specs=in_specs, out_specs=out_specs
        ),
        out_shape=out_shape,
        compiler_params=pltpu.CompilerParams(vmem_limit_bytes=VMEM_LIMIT),
        cost_estimate=pl.CostEstimate(flops=flops, bytes_accessed=moved, transcendentals=transcendentals),
    )


def whole(shape):
    return pl.BlockSpec(shape, lambda c, *_: (0,) * len(shape))


def tile(rows, width):
    return pl.BlockSpec((rows, width), lambda c, *_: (0, c))


def struct(shape, dtype):
    return jax.ShapeDtypeStruct(shape, dtype)


def in_hbm(shape, dtype):
    return pltpu.HBM(shape, dtype)


def matmul(left, right):
    return jnp.dot(left, right, preferred_element_type=F32)


def gate_values(tokens, halo, weight):
    x = tokens[...].astype(F32)
    row = lax.broadcasted_iota(jnp.int32, x.shape, 0)
    edge, taps = halo[...].astype(F32), weight[...]
    one_back = jnp.where(row == 0, edge[1:2], pltpu.roll(x, 1, 0))
    two_back = jnp.where(row == 0, edge[0:1], jnp.where(row == 1, edge[1:2], pltpu.roll(x, 2, 0)))
    conv = taps[0:1] * x + taps[1:2] * one_back + taps[2:3] * two_back
    return conv, jax.nn.sigmoid(conv)


def spread_peer_body(core, mine, other, values, piece, rows):
    half = mine.shape[0]
    ours, theirs = matmul(mine[...], values[...]).astype(BF16), matmul(other[...], values[...]).astype(BF16)

    @pl.when(core[0] == 0)
    def _():
        piece[0:half], piece[half:] = ours, theirs
        rows[0:half], rows[half:] = mine[...], other[...]

    @pl.when(core[0] != 0)
    def _():
        piece[0:half], piece[half:] = theirs, ours
        rows[0:half], rows[half:] = other[...], mine[...]


def spread_peer_call(core, mine, other, values):
    half, block = mine.shape
    channels = values.shape[1]
    width = channels
    return call(
        spread_peer_body,
        "spread_peer",
        (channels // width,),
        [whole((half, block))] * 2 + [tile(block, width)],
        [tile(2 * half, width), whole((2 * half, block))],
        [struct((2 * half, channels), BF16), struct((2 * half, block), BF16)],
        4 * half * block * channels,
        2 * block * channels + 8 * half * block,
        scalars=1,
    )(core, mine, other, values)


def spread_own_body(row, values, piece):
    piece[...] = matmul(row[...], values[...]).astype(BF16)


def spread_own_call(row, values):
    share, block = row.shape
    channels = values.shape[1]
    width = channels
    return call(
        spread_own_body,
        "spread_own",
        (channels // width,),
        [whole((share, block)), tile(block, width)],
        tile(share, width),
        struct((share, channels), BF16),
        2 * share * block * channels,
        2 * block * channels + 2 * share * (block + channels),
    )(row, values)


def spread_gated_body(peers, tokens, halo, weight, cot, *refs):
    rows, pieces = refs[:peers], refs[peers:]
    conv, sig = gate_values(tokens, halo, weight)
    gated = (cot[...].astype(F32) * (conv * sig)).astype(BF16)
    for row, piece in zip(rows, pieces):
        piece[...] = matmul(row[...], gated).astype(BF16)


def spread_gated_call(tokens, halo, weight, cot, rows):
    block, channels = tokens.shape
    peers, share = len(rows), rows[0].shape[0]
    width = min(channels, 128)
    out = call(
        functools.partial(spread_gated_body, peers),
        "spread_gated",
        (channels // width,),
        [tile(block, width), tile(2, width), tile(3, width), tile(block, width)]
        + [whole((share, block))] * peers,
        [tile(share, width)] * peers,
        [in_hbm((share, channels), BF16)] * peers,
        2 * peers * share * block * channels,
        4 * block * channels + 2 * peers * share * (block + channels),
        transcendentals=2 * block * channels,
    )(tokens, halo, weight, cot, *rows)
    return list(out)


def turn_body(peers, *refs):
    refs[peers][...] = join_rows(refs[:peers]).T


def turn_call(rows):
    share, block = rows[0].shape
    width = min(block, 256)
    return call(
        functools.partial(turn_body, len(rows)),
        "turn",
        (block // width,),
        [tile(share, width)] * len(rows),
        pl.BlockSpec((width, block), lambda c: (c, 0)),
        struct((block, block), BF16),
        block * block,
        4 * block * block,
    )(*rows)


def two_part(values):
    high = values.astype(BF16)
    return high, (values - high.astype(F32)).astype(BF16)


def middle_body(peers, span, with_grad, place, high, low, high_t, low_t, kern, *refs):
    pieces, refs = refs[:peers], refs[peers:]
    if with_grad:
        first, refs = refs[:peers], refs[peers:]
        grad, refs = refs[0], refs[1:]
    outs = refs[:peers]
    columns = pieces[0].shape[0]
    rows = [lax.bitwise_xor(place[0], r) for r in range(peers)]
    for g in range(columns // span):
        part = slice(g * span, (g + 1) * span)
        stacked = jnp.concatenate([piece[part] for piece in pieces], axis=0)
        mid = matmul(high[g], stacked) + matmul(low[g], stacked)
        if with_grad:
            stacked = jnp.concatenate([piece[part] for piece in first], axis=0)
            product = ((matmul(high[g], stacked) + matmul(low[g], stacked)) * mid).astype(BF16)
            for r in range(peers):
                grad[rows[r], part] = product[r * span : (r + 1) * span]
        filters = jnp.concatenate([kern[rows[r], part] for r in range(peers)], axis=0)
        upper, lower = two_part(filters.astype(F32) * mid)
        result = matmul(high_t[g], upper) + matmul(low_t[g], upper) + matmul(high_t[g], lower)
        result = result.astype(BF16)
        for r in range(peers):
            outs[r][part] = result[r * span : (r + 1) * span]


def middle_call(place, factors, kern, pieces, first=None):
    peers, columns, channels = kern.shape
    groups, side, _ = factors[0].shape
    width = min(channels, 256)
    cube = pl.BlockSpec((peers, columns, width), lambda c, *_: (0, 0, c))
    with_grad = first is not None
    n_in = peers * (2 if with_grad else 1)
    out = call(
        functools.partial(middle_body, peers, side // peers, with_grad),
        "middle_grad" if with_grad else "middle",
        (channels // width,),
        [whole((groups, side, side))] * 4 + [cube] + [tile(columns, width)] * n_in,
        ([cube] if with_grad else []) + [tile(columns, width)] * peers,
        ([struct(kern.shape, BF16)] if with_grad else []) + [in_hbm((columns, channels), BF16)] * peers,
        (14 if with_grad else 10) * groups * side * side * channels,
        (10 if with_grad else 6) * peers * columns * channels + 8 * groups * side * side,
        scalars=1,
    )(place, *factors, kern, *pieces, *(first or []))
    return (out[0], list(out[1:])) if with_grad else list(out)


def exact(left, right):
    return jnp.dot(left, right, precision=lax.Precision.HIGHEST, preferred_element_type=F32)


def factors_body(span, place, outer, twiddle, high, low, high_t, low_t):
    peers, columns = twiddle.shape
    side = peers * span

    def spots(shape, axis):
        return lax.broadcasted_iota(jnp.int32, shape, axis)

    pick = jnp.where(lax.bitwise_xor(spots((peers, peers), 0), place[0]) == spots((peers, peers), 1), 1.0, 0.0)
    spread_rows = jnp.where(lax.div(spots((side, peers), 0), span) == spots((side, peers), 1), 1.0, 0.0)
    owner = lax.div(spots((peers, side), 1), span) == spots((peers, side), 0)
    spread_columns = jnp.where(owner, 1.0, 0.0)
    outer_here = exact(pick, exact(outer[...], pick))
    twiddle_here = exact(pick, twiddle[...])
    wide = exact(exact(spread_rows, outer_here), spread_columns)
    same = lax.rem(spots((side, side), 0), span) == lax.rem(spots((side, side), 1), span)
    wide = jnp.where(same, wide, 0.0)
    for g in range(columns // span):
        at = lax.rem(spots((columns, side), 1), span) + g * span == spots((columns, side), 0)
        scale = exact(twiddle_here, jnp.where(at, 1.0, 0.0))
        scale = jnp.sum(jnp.where(owner, scale, 0.0), axis=0, keepdims=True)
        factor = wide * scale
        high[g], low[g] = two_part(factor)
        high_t[g], low_t[g] = two_part(factor.T)


def middle_factors(outer, twiddle, place):
    peers, columns = twiddle.shape
    span = min(columns, max(16, 256 // peers))
    groups, side = columns // span, peers * span
    shape = (groups, side, side)
    return call(
        functools.partial(factors_body, span),
        "factors",
        (1,),
        [whole(outer.shape), whole(twiddle.shape)],
        [whole(shape)] * 4,
        [struct(shape, BF16)] * 4,
        16 * groups * side * side,
        8 * groups * side * side,
        scalars=1,
    )(place, outer, twiddle)


def join_rows(pieces):
    return jnp.concatenate([piece[...] for piece in pieces], axis=0)


def forward_body(peers, turned, weight, tokens, halo, cot, *refs):
    pieces, (mixed, back, head) = refs[:peers], refs[peers:]
    conv_out = matmul(turned[...], join_rows(pieces))
    conv, sig = gate_values(tokens, halo, weight)
    mixed[...] = (conv * sig * conv_out).astype(BF16)
    slope = sig * (1.0 + conv * (1.0 - sig))
    grad = cot[...].astype(F32) * conv_out * slope
    head[...] = grad[0:2]
    length = grad.shape[0]
    row = lax.broadcasted_iota(jnp.int32, grad.shape, 0)
    taps = weight[...]
    one_on = jnp.where(row < length - 1, pltpu.roll(grad, length - 1, 0), 0.0)
    two_on = jnp.where(row < length - 2, pltpu.roll(grad, length - 2, 0), 0.0)
    back[...] = taps[0:1] * grad + taps[1:2] * one_on + taps[2:3] * two_on


def forward_call(turned, weight, tokens, halo, cot, pieces):
    length, channels = tokens.shape
    peers, share = len(pieces), pieces[0].shape[0]
    width = min(channels, 256)
    return call(
        functools.partial(forward_body, peers),
        "forward_rows",
        (channels // width,),
        [whole(turned.shape), tile(3, width), tile(length, width), tile(2, width), tile(length, width)]
        + [tile(share, width)] * peers,
        [tile(length, width), tile(length, width), tile(2, width)],
        [struct((length, channels), BF16), struct((length, channels), F32), struct((2, channels), F32)],
        2 * length * length * channels,
        12 * length * channels + 2 * length * length,
        transcendentals=2 * length * channels,
    )(turned, weight, tokens, halo, cot, *pieces)


def in_vmem(count):
    return [pl.BlockSpec(memory_space=pltpu.VMEM)] * count


def partial_body(peers, width, turned, back, *refs):
    pieces, total = refs[:peers], refs[peers]
    depth = peers * pieces[0].shape[0]
    for c in range(total.shape[1] // width):
        part = slice(c * width, (c + 1) * width)
        stacked = jnp.concatenate([piece[:, part] for piece in pieces], axis=0)
        total[:, part] = matmul(turned[:, :depth], stacked) + back[:, part]


def partial_call(turned, back, pieces):
    length, channels = back.shape
    depth = len(pieces) * pieces[0].shape[0]
    return pl.pallas_call(
        functools.partial(partial_body, len(pieces), min(channels, 256)),
        name="backward_part",
        in_specs=in_vmem(2 + len(pieces)),
        out_specs=in_vmem(1)[0],
        out_shape=struct((length, channels), F32),
        compiler_params=pltpu.CompilerParams(vmem_limit_bytes=8 * MIB),
        cost_estimate=pl.CostEstimate(
            flops=2 * length * depth * channels, bytes_accessed=8 * length * channels, transcendentals=0
        ),
    )(turned, back, *pieces)


def backward_body(peers, width, turned, weight, back, tail, *refs):
    pieces, out, made, sems = refs[:peers], refs[peers], refs[peers + 1], refs[peers + 2]
    length, channels = made.shape
    depth = peers * pieces[0].shape[0]
    copies = []
    for c in range(channels // width):
        part = slice(c * width, (c + 1) * width)
        stacked = jnp.concatenate([piece[:, part] for piece in pieces], axis=0)
        total = matmul(turned[:, turned.shape[1] - depth :], stacked) + back[:, part]
        taps, edge = weight[:, part], tail[:, part]
        made[: length - 16, part] = total[: length - 16].astype(BF16)
        last = total[length - 16 :]
        row = lax.broadcasted_iota(jnp.int32, last.shape, 0)
        extra = jnp.where(row == 15, taps[1:2] * edge[0:1] + taps[2:3] * edge[1:2], 0.0)
        extra = jnp.where(row == 14, taps[2:3] * edge[0:1], extra)
        made[length - 16 :, part] = (last + extra).astype(BF16)
        copies.append(pltpu.make_async_copy(made.at[:, part], out.at[:, part], sems.at[c]))
        copies[-1].start()
    for copy in copies:
        copy.wait()


def backward_call(turned, weight, back, tail, pieces):
    length, channels = back.shape
    peers, depth = len(pieces), len(pieces) * pieces[0].shape[0]
    width = min(channels, 256)
    return pl.pallas_call(
        functools.partial(backward_body, peers, width),
        name="backward_rows",
        in_specs=in_vmem(4 + peers),
        out_specs=pl.BlockSpec(memory_space=pl.ANY),
        out_shape=struct((length, channels), BF16),
        scratch_shapes=[
            pltpu.VMEM((length, channels), BF16),
            pltpu.SemaphoreType.DMA((channels // width,)),
        ],
        compiler_params=pltpu.CompilerParams(vmem_limit_bytes=8 * MIB),
        cost_estimate=pl.CostEstimate(
            flops=2 * length * depth * channels, bytes_accessed=6 * length * channels, transcendentals=0
        ),
    )(turned, weight, back, tail, *pieces)


def after(value, *others):
    return lax.optimization_barrier((value, *others))[0]


class Wire:
    DEPTH = 5

    def __init__(self):
        self.ended = []

    def exchange(self, block, mask):
        if len(self.ended) >= self.DEPTH:
            block = after(block, self.ended[-self.DEPTH])
        self.ended.append(exchange(block, mask))
        return self.ended[-1]


def on_device(tokens, short_weight, inner_factor, outer_factor, twiddle, kernel, cotangent):
    peers = lax.axis_size("seq")
    place, core = lax.axis_index("seq"), lax.axis_index("ch")
    row_count, block, channels = tokens.shape
    assert row_count == 1 and lax.axis_size("ch") == 2
    flat, cot = tokens.reshape(block, channels), cotangent.reshape(block, channels)
    share = inner_factor.shape[0]
    place_ref, core_ref = place.reshape(1).astype(jnp.int32), core.reshape(1).astype(jnp.int32)
    assert peers & (peers - 1) == 0
    far = peers // 2
    others = [far] + [m for pair in zip(range(1, far), range(far + 1, peers)) for m in pair]
    arrival = [0] + others
    wire = Wire()

    half = lax.dynamic_slice(inner_factor, (core * (share // 2), 0), (share // 2, block))
    mine = {far: wire.exchange(half, far)}
    for m in range(1, far):
        mine[m] = wire.exchange(half, m)
    preceding = shifted(flat[-2:], 1)
    for m in range(1, far):
        mine[far + m] = wire.exchange(mine[far], m)

    rows, spread, pieces = {0: inner_factor}, {}, []
    for m in others:
        piece, rows[m] = spread_peer_call(core_ref, mine[m], swap_cores(mine[m]), flat)
        pieces.append(piece)
        spread[m] = wire.exchange(piece, m)
    held = after(flat, pieces[-1])
    spread[0] = spread_own_call(inner_factor, held)

    in_order = [rows[m] for m in range(peers)]
    spread_cot = spread_gated_call(held, preceding, short_weight, cot, in_order)
    factors = middle_factors(after(outer_factor, spread_cot[0]), twiddle, place_ref)
    spread_cot = {m: wire.exchange(spread_cot[m], m) for m in others} | {0: spread_cot[0]}
    turned = turn_call([rows[m] for m in arrival])

    spread = [spread[m] for m in range(peers)]
    mid = middle_call(place_ref, factors, kernel, spread)
    rows_fwd = {m: wire.exchange(mid[m], m) for m in others} | {0: mid[0]}
    spread_cot[0] = after(spread_cot[0], mid[0])
    kernel_grad, mid = middle_call(place_ref, factors, kernel, [spread_cot[m] for m in range(peers)], spread)
    rows_bwd = {0: mid[0]}
    for m in others[:-2]:
        rows_bwd[m] = wire.exchange(mid[m], m)
    mixer_out, back, head = forward_call(
        turned, short_weight, flat, preceding, cot, [rows_fwd[m] for m in arrival]
    )
    following = shifted(head, -1)
    for m in others[-2:]:
        rows_bwd[m] = wire.exchange(after(mid[m], head), m)
    late = max(1, peers // 4)
    back = partial_call(turned, back, [rows_bwd[m] for m in arrival[:-late]])
    token_grad = backward_call(turned, short_weight, back, following, [rows_bwd[m] for m in arrival[-late:]])
    return mixer_out.reshape(tokens.shape), token_grad.reshape(tokens.shape), kernel_grad


def solution(mesh):
    in_specs = (
        P(("grp", "seq"), None, "ch"),
        P(None, "ch"),
        P("seq", None),
        P(),
        P(None, "seq"),
        P(None, "seq", "ch"),
        P(("grp", "seq"), None, "ch"),
    )
    out_specs = (
        P(("grp", "seq"), None, "ch"),
        P(("grp", "seq"), None, "ch"),
        P("grp", "seq", "ch"),
    )
    return jax.shard_map(
        on_device, mesh=mesh, in_specs=in_specs, out_specs=out_specs, check_vma=False
    )
```
